32 devices in a mesh: obs: 4 (over x, core), ord: 8 (over z, y).
Axes of the slice: x: 2, y: 2, z: 4, core: 2. Of those that a mesh axis runs over, the one named last changes fastest.
Arguments:
- longitude: float32 [4, 32768], P('obs'), may hold values from -3.140625 to 3.140625
- cycle_of: int32 [4, 32768], P('obs'), may hold values from 0 to 255, never falling along the last dimension, each value on 1 to 256 neighbouring positions
- obs_count: int32 [4], P('obs'), may hold values from 16384 to 32768
- observed: float32 [4, 32768], P('obs'), may hold values from -896 to 896
- obs_weight: float32 [4, 32768], P('obs'), may hold values from 0.3 to 3
- legendre: float32 [4, 72, 288, 256], P('obs', 'ord'), as said below
- precond_inv: float32 [72, 288, 288], P('ord'), as said below
- order_of_slot: int32 [72], P('ord'), may hold values from 0 to 71, each once
Outputs:
- solution: float32 [72, 2, 288], P('ord')
- residual: float32 [72, 2, 288], P('ord')
The draws below stay inside these ranges and needn't reach their ends.
Inputs may be any that keep to these rules, and one draw needn't show every extreme that they name: `cycle_of`: cycle numbers never fall along a slab; each cycle holds at least one observation slot. `obs_count`: observation slots at or beyond a slab's count carry no weight. legendre[b, m, n, j] is the fully normalized associated Legendre function of degree n and order m at the colatitude of cycle j of slab b, and 0 for n < m. `precond_inv`: every block is symmetric positive definite. order_of_slot names each order once; slot s lies on ord index s // 9.
All inputs are finite; a program needn't handle non-finite values.
Results may differ from the reference program's by a relative error of at most 0.0003.
Values sent between devices are 32-bit elements; how exact they have to be, the bound alone decides.
No kernel may reach another device: no remote copies, remote signals or barrier semaphores. Data moves between devices by JAX's collectives and lax.ppermute only.
A program may use at most 128 MiB of HBM per device.

```python
import math
import jax
import jax.numpy as jnp
import numpy as np
from jax import lax

NB = 288
CYCLE_DEV = 256
OBS_DEV = 32768
ITERS = 2
ORDERS = 72
N_OBS = 4


def draw_legendre(key, part):
    colatitude = jax.random.uniform(jax.random.fold_in(key, 11), (N_OBS, CYCLE_DEV), jnp.float32, 0.25, 2.89)
    cosine_col = jnp.cos(colatitude)[:, :, None]
    sine_col = jnp.sin(colatitude)[:, :, None]
    orders = jnp.arange(ORDERS, dtype=jnp.int32).astype(jnp.float32)
    gamma_log = jax.scipy.special.gammaln
    log_start = 0.5 * (gamma_log(2.0 * orders + 2.0) - orders * jnp.log(4.0) - 2.0 * gamma_log(orders + 1.0))
    log_start = log_start + 0.5 * jnp.log(jnp.where(orders > 0, 2.0, 1.0))
    sectoral = jnp.exp(orders[None, None, :] * jnp.log(sine_col) + log_start[None, None, :])
    zeros = jnp.zeros((N_OBS, CYCLE_DEV, ORDERS), jnp.float32)

    def degree_step(state_pair, degree):
        previous, before_previous = state_pair
        degree_f = degree.astype(jnp.float32)
        minus_order = jnp.maximum(degree_f - orders, 1.0)
        plus_order = jnp.maximum(degree_f + orders, 1.0)
        rise_factor = jnp.sqrt(jnp.maximum((2.0 * degree_f - 1.0) * (2.0 * degree_f + 1.0), 0.0) / (minus_order * plus_order))
        fall_top = jnp.maximum((2.0 * degree_f + 1.0) * (degree_f + orders - 1.0) * (degree_f - orders - 1.0), 0.0)
        fall_factor = jnp.sqrt(fall_top / (minus_order * plus_order * jnp.maximum(2.0 * degree_f - 3.0, 1.0)))
        recurred = rise_factor * cosine_col * previous - fall_factor * before_previous
        current = jnp.where(degree_f < orders, 0.0, jnp.where(degree_f == orders, sectoral, recurred))
        return ((current, previous), current)
    unused, values = lax.scan(degree_step, (zeros, zeros), jnp.arange(NB, dtype=jnp.int32))
    return jnp.transpose(values, (1, 3, 0, 2))


def draw_precond_inv(key, part):
    diag_key, noise_key = jax.random.split(jax.random.fold_in(key, 23))
    diagonal = jnp.exp(jax.random.uniform(diag_key, (ORDERS, NB), jnp.float32, 0.0, jnp.log(4.0)))
    random_part = jax.random.normal(noise_key, (ORDERS, NB, NB), jnp.float32) * (0.18 / NB ** 0.5)
    symmetric = (random_part + jnp.transpose(random_part, (0, 2, 1))) / jnp.sqrt(2.0)
    root_diag = jnp.sqrt(diagonal)
    unit = jnp.eye(NB, dtype=jnp.float32)
    return (unit[None, :, :] + symmetric) * root_diag[:, :, None] * root_diag[:, None, :]


def with_ends(drawn, key, least, largest):
    longest = drawn.shape.index(max(drawn.shape))
    spots = []
    for shift in (0, 1):
        where = [jax.random.randint(jax.random.fold_in(key, axis), (), 0, length) for axis, length in enumerate(drawn.shape)]
        where[longest] = (where[longest] + shift) % drawn.shape[longest]
        spots.append(tuple(where))
    return drawn.at[spots[0]].set(least).at[spots[1]].set(largest)


def shard_levels(key, shape, cuts, smallest, top_value):
    factor_of = 1.0
    for position, blocks in cuts:
        steps = jax.random.uniform(jax.random.fold_in(jax.random.fold_in(key, 6), position), (blocks,), jnp.float32, smallest / len(cuts), top_value / len(cuts))
        factor_of = factor_of * jnp.repeat(jnp.exp(steps), shape[position] // blocks).reshape((-1,) + (1,) * (len(shape) - 1 - position))
    return factor_of


def profile(number_of, total, bound, lean):
    loads = [(1 << 20) // math.isqrt(rank ** lean) + 1 for rank in range(2, number_of + 1)]
    rest, given = total - bound - (number_of - 1), [1] * (number_of - 1)
    while rest > 0:
        candidates = [i for i in range(number_of - 1) if given[i] < bound]
        mass, left = sum([loads[i] for i in candidates]), rest
        for i in candidates:
            more = min(bound - given[i], max(1, left * loads[i] // mass), rest)
            given[i] = given[i] + more
            rest = rest - more
    return np.array([bound] + given)


def ragged(key, count, total, limit, lean):
    if count == 2:
        one = jax.random.randint(key, (), max(1, total - limit), min(limit, total - 1) + 1)
        return jnp.stack([one, total - one])
    lengths = jnp.asarray(profile(count, total, limit, lean), jnp.int32)
    couples = (count - 1) // 2
    source_of, sink = lengths[1:1 + 2 * couples:2], lengths[2:2 + 2 * couples:2]
    slack = jnp.minimum(source_of - 1, limit - sink)
    moved = jax.random.randint(jax.random.fold_in(key, 1), (couples,), 0, 1 << 20) % (slack + 1)
    lengths = lengths.at[1:1 + 2 * couples:2].set(source_of - moved).at[2:2 + 2 * couples:2].set(sink + moved)
    return lengths[jax.random.permutation(jax.random.fold_in(key, 2), count)]


def scatter_about(rng, shape, width, limit, cuts=(), held_as=jnp.bfloat16):
    loudness = shard_levels(rng, shape, cuts, -0.22, 0.18) if cuts else 1.0
    drawn = jax.random.normal(rng, shape, jnp.float32) * width * loudness
    return jnp.minimum(jnp.maximum(drawn, -limit), limit).astype(held_as)


def setup_inputs(seed: int = 0) -> dict:
    key_of = jax.random.split(jax.random.key(seed), 9)
    longitude = jnp.clip(jax.random.uniform(key_of[0], (N_OBS, OBS_DEV), jnp.float32, -3.140625, 3.140625), -3.140625, 3.140625)
    cycle_of = jax.vmap(lambda own: jnp.searchsorted(jnp.cumsum(ragged(own, CYCLE_DEV, OBS_DEV, 2 * OBS_DEV // CYCLE_DEV, 1)), jnp.arange(OBS_DEV), side="right"))(jax.random.split(key_of[1], N_OBS)).reshape((N_OBS, OBS_DEV)).astype(jnp.int32)
    obs_count = with_ends(jax.random.randint(key_of[2], (N_OBS,), OBS_DEV // 2, OBS_DEV + 1), jax.random.fold_in(key_of[2], 1), OBS_DEV // 2, OBS_DEV).astype(jnp.int32)
    observed = scatter_about(key_of[3], (N_OBS, OBS_DEV), ((ORDERS * NB) ** 0.5), 896.0, ((0, 4),), jnp.float32)
    obs_weight = jnp.clip(jnp.exp(math.log(3.0) - 2.3025851 * jax.random.uniform(key_of[4], (N_OBS, OBS_DEV), jnp.float32) ** shard_levels(key_of[4], (N_OBS, OBS_DEV), ((0, 4),), -0.2, 0.2)), 0.3, 3.0)
    legendre = draw_legendre(jax.random.fold_in(key_of[8], 71), 0)
    precond_inv = draw_precond_inv(jax.random.fold_in(key_of[8], 71), 0)
    order_of_slot = jax.random.permutation(key_of[7], ORDERS).astype(jnp.int32)
    return {"longitude": longitude, "cycle_of": cycle_of, "obs_count": obs_count, "observed": observed, "obs_weight": obs_weight, "legendre": legendre, "precond_inv": precond_inv, "order_of_slot": order_of_slot}


PRECISE = lax.Precision.HIGHEST


def harmonic_table(orders, longitudes):
    angles = orders.astype(jnp.float32)[:, None] * longitudes[None, :]
    return jnp.stack([jnp.cos(angles), jnp.sin(angles)], axis=1)


def synthesize(coefficients, legendre_here, harmonic, cycle_ids):
    cycle_values = jnp.einsum("okn,onr->okr", coefficients, legendre_here, precision=PRECISE)
    at_points = jnp.take(cycle_values, cycle_ids, axis=2)
    return jnp.sum(at_points * harmonic, axis=(0, 1))


def adjoint(values, legendre_here, harmonic, cycle_ids):
    weighted = harmonic * values[None, None, :]
    per_cycle = jax.ops.segment_sum(jnp.moveaxis(weighted, 2, 0), cycle_ids, num_segments=legendre_here.shape[2], indices_are_sorted=True)
    return jnp.einsum("rok,onr->okn", per_cycle, legendre_here, precision=PRECISE)


def reference(longitude, cycle_of, obs_count, observed, obs_weight, legendre, precond_inv, order_of_slot):
    orders = jnp.arange(ORDERS, dtype=jnp.int32)
    slot_of_order = jnp.sum(jnp.where(order_of_slot[None, :] == orders[:, None], orders[None, :], 0), axis=1).astype(jnp.int32)
    live_mask = (jnp.arange(NB, dtype=jnp.int32)[None, None, :] >= order_of_slot[:, None, None]).astype(jnp.float32)
    positions = jnp.arange(OBS_DEV, dtype=jnp.int32)
    obs_scale = obs_weight * (positions[None, :] < obs_count[:, None]).astype(jnp.float32) / (N_OBS * OBS_DEV)

    def owner_adjoint(values):
        def slab_step(accumulated, slab_data):
            east, cycle_ids, slab_values, legendre_here = slab_data
            harmonic = harmonic_table(orders, east)
            return accumulated + adjoint(slab_values, legendre_here, harmonic, cycle_ids), None

        accumulated, unused = lax.scan(slab_step, jnp.zeros((ORDERS, 2, NB), jnp.float32), (longitude, cycle_of, values, legendre))
        return jnp.take(accumulated, order_of_slot, axis=0)

    def normal_image(direction):
        coefficients = jnp.take(direction, slot_of_order, axis=0)

        def slab_step(accumulated, slab_data):
            east, cycle_ids, slab_scale, legendre_here = slab_data
            harmonic = harmonic_table(orders, east)
            gradient = synthesize(coefficients, legendre_here, harmonic, cycle_ids)
            return accumulated + adjoint(slab_scale * gradient, legendre_here, harmonic, cycle_ids), None

        accumulated, unused = lax.scan(slab_step, jnp.zeros((ORDERS, 2, NB), jnp.float32), (longitude, cycle_of, obs_scale, legendre))
        return jnp.take(accumulated, order_of_slot, axis=0)

    def precondition(values):
        return live_mask * jnp.einsum("snj,skj->skn", precond_inv, values, precision=PRECISE)

    residual = owner_adjoint(obs_scale * observed)
    solution = jnp.zeros_like(residual)
    precond = precondition(residual)
    direction = precond
    energy_now = jnp.sum(residual * precond)
    for iteration in range(ITERS):
        image = normal_image(direction)
        step_size = energy_now / jnp.sum(direction * image)
        solution = solution + step_size * direction
        residual = residual - step_size * image
        if iteration + 1 < ITERS:
            precond = precondition(residual)
            energy_next = jnp.sum(residual * precond)
            direction = precond + (energy_next / energy_now) * direction
            energy_now = energy_next
    return solution, residual
```

```python
import functools

import jax
import jax.numpy as jnp
from jax import lax
from jax.experimental import pallas as pl
from jax.experimental.pallas import tpu as pltpu
from jax.sharding import PartitionSpec as P

ITERS = 2
SEGMENTS = 2
CHUNK = 1024
F32 = jnp.float32
BF16 = jnp.bfloat16

VMEM = pl.BlockSpec(memory_space=pltpu.VMEM)
SMEM = pl.BlockSpec(memory_space=pltpu.SMEM)


def up(value, unit):
    return -(-value // unit) * unit


def iota(shape, axis):
    return lax.broadcasted_iota(jnp.int32, shape, axis)


class Sizes:
    def __init__(self, legendre, slab):
        self.cnt, self.nb, self.cyc = legendre.shape[1:]
        self.nord = lax.axis_size("ord")
        self.nobs = lax.axis_size("obs")
        self.no = self.cnt * self.nord
        self.slab = slab
        self.rows = slab // 128
        self.halves = self.cyc // 128
        self.steps = self.nb // 8
        per = 128 // self.steps
        while self.cnt % per or per * self.steps == 128:
            per -= 1
        self.per = per
        self.groups = self.cnt // per
        self.tiles = 2 * self.groups
        self.seg = SEGMENTS
        self.seg_len = self.nb // SEGMENTS
        self.seed_rows = 2 * self.seg + 1
        self.id_row = self.cnt * self.seed_rows
        self.seeds = up(self.id_row + 1, 8)
        self.pay = up(2 * self.cnt + 1, 8)
        self.off = up(self.no, 8)
        self.freq = up(2 * self.no - 1, 16)
        self.table = self.off + self.freq
        self.own = up(self.cnt, 16)


def seeds_kernel(z, first_ref, own_ref, leg_ref, out_ref, keep):
    i = pl.program_id(0)
    base = i * z.seed_rows
    for s in range(z.seg):
        for t in range(2):
            keep[pl.ds(base + 2 * s + t, 1), :] = leg_ref[0, 0, s * z.seg_len + t : s * z.seg_len + t + 1, :]
    order = first_ref[0] + i
    keep[pl.ds(base + 2 * z.seg, 1), :] = leg_ref[0, 0, pl.ds(order, 1), :]

    @pl.when(i == z.cnt - 1)
    def _():
        lane = iota((z.seeds - z.id_row, z.cyc), 1)
        ids = jnp.zeros(lane.shape, F32)
        for slot in range(z.cnt):
            ids = jnp.where(lane == slot, own_ref[slot].astype(F32), ids)
        keep[z.id_row :, :] = ids
        for d in range(z.nord):
            out_ref[d] = keep[...]


def make_seeds(z, first, own, legendre):
    return pl.pallas_call(
        functools.partial(seeds_kernel, z),
        grid=(z.cnt,),
        in_specs=[SMEM, SMEM, pl.BlockSpec((1, 1, z.nb, z.cyc), lambda i: (0, i, 0, 0))],
        out_specs=pl.BlockSpec((z.nord, z.seeds, z.cyc), lambda i: (0, 0, 0)),
        out_shape=jax.ShapeDtypeStruct((z.nord, z.seeds, z.cyc), F32),
        scratch_shapes=[pltpu.VMEM((z.seeds, z.cyc), F32)],
        name="seeds",
    )(first, own, legendre)


def sincos(angle):
    turn = jnp.round(angle * 0.6366197723675814)
    rest = angle - turn * 1.5703125
    rest = rest - turn * 4.837512969970703e-4
    rest = rest - turn * 7.549789948768648e-8
    sq = rest * rest
    sine = rest + rest * sq * (-0.16666654611 + sq * (8.3321608736e-3 + sq * -1.9515295891e-4))
    cosine = 1.0 - 0.5 * sq + sq * sq * (4.166664568298827e-2 + sq * (-1.388731625493765e-3 + sq * 2.443315711809948e-5))
    quarter = turn.astype(jnp.int32)
    odd = (quarter & 1) == 1
    c = jnp.where(odd, sine, cosine)
    s = jnp.where(odd, cosine, sine)
    c = jnp.where(((quarter + 1) & 2) == 2, -c, c)
    s = jnp.where((quarter & 2) == 2, -s, s)
    return c, s


def split(value):
    high = value.astype(BF16)
    return high, (value - high.astype(F32)).astype(BF16)


def tables_kernel(z, count_ref, own_ref, lon_ref, cyc_ref, data_ref, weight_ref, tc_ref, ts_ref, ty_ref,
                  bc, bs, yc, ys, c8, s8, lhs, hot, acc):
    total = z.slab * z.nobs
    lon = lon_ref[...]
    place = iota((z.rows, 128), 0) * 128 + iota((z.rows, 128), 1)
    scale = weight_ref[...] * (place < count_ref[0]).astype(F32) / total
    c1, s1 = sincos(lon)
    cp, sp = c1, s1
    bc[0 : z.rows, :] = scale
    bs[0 : z.rows, :] = jnp.zeros_like(scale)
    for p in range(1, 8):
        bc[p * z.rows : (p + 1) * z.rows, :] = scale * cp
        bs[p * z.rows : (p + 1) * z.rows, :] = scale * sp
        cp, sp = cp * c1 - sp * s1, sp * c1 + cp * s1
    c8[...] = cp
    s8[...] = sp
    scaled = scale * data_ref[...]

    def own_order(i, carry):
        c, s = sincos(own_ref[i].astype(F32) * lon_ref[...])
        yc[pl.ds(pl.multiple_of(i * z.rows, 8), z.rows), :] = c * scaled
        ys[pl.ds(pl.multiple_of(i * z.rows, 8), z.rows), :] = s * scaled
        return carry

    lax.fori_loop(0, z.cnt, own_order, 0)
    for i in range(z.cnt, z.own):
        yc[i * z.rows : (i + 1) * z.rows, :] = jnp.zeros_like(lon)
        ys[i * z.rows : (i + 1) * z.rows, :] = jnp.zeros_like(lon)
    acc[...] = jnp.zeros_like(acc)
    cycle_id = iota((z.cyc, 128), 0)
    top = 4 * z.freq
    width = min(CHUNK, z.slab) // 128

    def chunk(step, carry):
        for k in range(width):
            r = step * width + k
            lanes = slice(k * 128, (k + 1) * 128)
            c = bc[pl.ds(r, 8, stride=z.rows), :]
            s = bs[pl.ds(r, 8, stride=z.rows), :]
            cr = jnp.broadcast_to(c8[pl.ds(r, 1), :], (8, 128))
            sr = jnp.broadcast_to(s8[pl.ds(r, 1), :], (8, 128))
            for pair in range(z.freq // 16):
                c2 = c * cr - s * sr
                s2 = s * cr + c * sr
                high, low = split(jnp.concatenate([c, c2], 0))
                lhs[pair * 16 : pair * 16 + 16, lanes] = high
                lhs[z.freq + pair * 16 : z.freq + pair * 16 + 16, lanes] = low
                high, low = split(jnp.concatenate([s, s2], 0))
                lhs[2 * z.freq + pair * 16 : 2 * z.freq + pair * 16 + 16, lanes] = high
                lhs[3 * z.freq + pair * 16 : 3 * z.freq + pair * 16 + 16, lanes] = low
                c = c2 * cr - s2 * sr
                s = s2 * cr + c2 * sr
            for part, table in enumerate((yc, ys)):
                for block in range(z.own // 16):
                    a = table[pl.ds(block * 16 * z.rows + r, 8, stride=z.rows), :]
                    b = table[pl.ds((block * 16 + 8) * z.rows + r, 8, stride=z.rows), :]
                    high, low = split(jnp.concatenate([a, b], 0))
                    at = top + 2 * part * z.own + block * 16
                    lhs[at : at + 16, lanes] = high
                    lhs[at + z.own : at + z.own + 16, lanes] = low
            hot[:, lanes] = jnp.where(cycle_id == cyc_ref[pl.ds(r, 1), :], 1.0, 0.0).astype(BF16)
        acc[...] += lax.dot_general(lhs[...], hot[...], (((1,), (1,)), ((), ())), preferred_element_type=F32)
        return carry

    lax.fori_loop(0, z.rows // width, chunk, 0)
    for h in range(z.halves):
        lanes = slice(h * 128, (h + 1) * 128)
        tc_ref[h, z.off :, :] = acc[0 : z.freq, lanes] + acc[z.freq : 2 * z.freq, lanes]
        ts_ref[h, z.off :, :] = acc[2 * z.freq : 3 * z.freq, lanes] + acc[3 * z.freq : 4 * z.freq, lanes]

    def mirror(q, carry):
        for h in range(z.halves):
            tc_ref[h, pl.ds(z.off - q, 1), :] = tc_ref[h, pl.ds(z.off + q, 1), :]
            ts_ref[h, pl.ds(z.off - q, 1), :] = -ts_ref[h, pl.ds(z.off + q, 1), :]
        return carry

    lax.fori_loop(1, z.no, mirror, 0)
    for part in range(2):
        at = top + 2 * part * z.own
        for h in range(z.halves):
            lanes = slice(h * 128, (h + 1) * 128)
            ty_ref[h, part * z.cnt : (part + 1) * z.cnt, :] = (
                acc[at : at + z.cnt, lanes] + acc[at + z.own : at + z.own + z.cnt, lanes]
            )


def make_tables(z, count, own, lon, cyc, data, weight):
    lhs_rows = 4 * z.freq + 4 * z.own
    table = jax.ShapeDtypeStruct((z.halves, z.table, 128), F32)
    return pl.pallas_call(
        functools.partial(tables_kernel, z),
        in_specs=[SMEM, SMEM] + [VMEM] * 4,
        out_specs=[VMEM] * 3,
        out_shape=[table, table, jax.ShapeDtypeStruct((z.halves, z.pay, 128), F32)],
        scratch_shapes=[pltpu.VMEM((8 * z.rows, 128), F32)] * 2
        + [pltpu.VMEM((z.own * z.rows, 128), F32)] * 2
        + [pltpu.VMEM((z.rows, 128), F32)] * 2
        + [
            pltpu.VMEM((lhs_rows, min(CHUNK, z.slab)), BF16),
            pltpu.VMEM((z.cyc, min(CHUNK, z.slab)), BF16),
            pltpu.VMEM((lhs_rows, z.cyc), F32),
        ],
        name="tables",
    )(count, own, lon, cyc, data, weight)


def adjoint_into(z, func_ref, rows_ref, out_ref):
    lane = iota((8, 128), 1)

    def group(g, carry):
        tiles = [jnp.zeros((8, 128), F32)] * 2
        for p in range(z.per):
            slot = g * z.per + p
            w = [
                [
                    jnp.broadcast_to(rows_ref[h, pl.ds(k * z.cnt + slot, 1), :], (8, 128))
                    for h in range(z.halves)
                ]
                for k in range(2)
            ]
            for a in range(z.steps):
                at = pl.multiple_of(slot * z.nb + 8 * a, 8)
                f = [func_ref[h, pl.ds(at, 8), :] for h in range(z.halves)]
                for k in range(2):
                    prod = f[0] * w[k][0]
                    for h in range(1, z.halves):
                        prod = prod + f[h] * w[k][h]
                    tiles[k] = jnp.where(lane == p * z.steps + a, jnp.sum(prod, axis=1, keepdims=True), tiles[k])
        for k in range(2):
            out_ref[k * z.groups + g] = tiles[k]
        return carry

    lax.fori_loop(0, z.groups, group, 0)


def functions_kernel(z, own_ref, recv_ref, ty_ref, func_ref, out_ref, seed0, seed1, first):
    total = z.seg * z.cnt
    padded = up(total, 8)
    for slot in range(z.cnt):
        order = own_ref[slot]
        block = order // z.cnt
        base = (order - block * z.cnt) * z.seed_rows
        for s in range(z.seg):
            r = slot * z.seg + s
            seed0[r : r + 1, :] = recv_ref[block, pl.ds(base + 2 * s, 1), :]
            seed1[r : r + 1, :] = recv_ref[block, pl.ds(base + 2 * s + 1, 1), :]
            first[r : r + 1, :] = recv_ref[block, pl.ds(base + 2 * z.seg, 1), :]
    cosine = recv_ref[0, 1:2, :] / (recv_ref[0, 0:1, :] * 1.7320508075688772)
    lanes_len = up(z.seg_len, 128)
    row = iota((padded, lanes_len), 0)
    order_of = jnp.zeros(row.shape, F32)
    degree = jnp.zeros(row.shape, F32) + iota(row.shape, 1).astype(F32)
    for slot in range(z.cnt):
        for s in range(z.seg):
            hit = row == slot * z.seg + s
            order_of = jnp.where(hit, own_ref[slot].astype(F32), order_of)
            degree = jnp.where(hit, degree + float(s * z.seg_len), degree)
    minus = jnp.maximum(degree - order_of, 1.0)
    plus = jnp.maximum(degree + order_of, 1.0)
    rise = jnp.sqrt(jnp.maximum((2.0 * degree - 1.0) * (2.0 * degree + 1.0), 0.0) / (minus * plus))
    rise = jnp.where(degree > order_of, rise, 0.0)
    top = jnp.maximum((2.0 * degree + 1.0) * (degree + order_of - 1.0) * (degree - order_of - 1.0), 0.0)
    fall = jnp.sqrt(top / (minus * plus * jnp.maximum(2.0 * degree - 3.0, 1.0)))
    fall = jnp.where(degree > order_of + 1.0, fall, 0.0)
    starts = (degree == order_of).astype(F32)
    for h in range(z.halves):
        lanes = slice(h * 128, (h + 1) * 128)
        x = jnp.broadcast_to(cosine[:, lanes], (8, 128))
        for tile in range(padded // 8):
            rows = slice(tile * 8, tile * 8 + 8)
            left = min(8, total - tile * 8)
            before, prev = None, None
            for t in range(z.seg_len):
                if t == 0:
                    now = seed0[rows, lanes]
                elif t == 1:
                    now = seed1[rows, lanes]
                else:
                    now = (rise[rows, t : t + 1] * x) * prev - fall[rows, t : t + 1] * before
                    now = jnp.where(starts[rows, t : t + 1] > 0.5, first[rows, lanes], now)
                func_ref[h, pl.ds(tile * 8 * z.seg_len + t, left, stride=z.seg_len), :] = now[:left]
                before, prev = prev, now
    adjoint_into(z, func_ref, ty_ref, out_ref)


def make_functions(z, own, recv, ty):
    padded = up(z.seg * z.cnt, 8)
    return pl.pallas_call(
        functools.partial(functions_kernel, z),
        in_specs=[SMEM, VMEM, VMEM],
        out_specs=[VMEM] * 2,
        out_shape=[
            jax.ShapeDtypeStruct((z.halves, z.cnt * z.nb, 128), F32),
            jax.ShapeDtypeStruct((z.tiles, 8, 128), F32),
        ],
        scratch_shapes=[pltpu.VMEM((padded, z.cyc), F32)] * 3,
        name="functions",
    )(own, recv, ty)


def total_of(z, gathered_ref):
    summed = [gathered_ref[0, t] for t in range(z.tiles)]
    for b in range(1, z.nobs):
        summed = [summed[t] + gathered_ref[b, t] for t in range(z.tiles)]
    lane = iota((8, 128), 1)
    curvature = jnp.max(jnp.where((lane == 127) & (iota((8, 128), 0) == 0), summed[0], -jnp.inf), axis=1, keepdims=True)
    curvature = jnp.max(curvature, axis=0, keepdims=True)
    used = lane < z.per * z.steps
    return [jnp.where(used, s, 0.0) for s in summed], curvature


def full_sum(value):
    return jnp.sum(jnp.sum(value, axis=1, keepdims=True), axis=0, keepdims=True)


def step_kernel(z, later, own_ref, *refs):
    if later:
        gathered_ref, inv_ref, func_ref, energy_ref, res_ref, dir_ref = refs[:6]
        out_ref, newres_ref, prec_ref, sol_ref, flat = refs[6:]
    else:
        gathered_ref, inv_ref, func_ref = refs[:3]
        out_ref, newres_ref, prec_ref, flat = refs[3:]
    summed, curvature = total_of(z, gathered_ref)
    if later:
        step_size = energy_ref[0:1, 0:1] / curvature
        for t in range(z.tiles):
            sol_ref[t] = step_size * dir_ref[t]
            newres_ref[t] = res_ref[t] - step_size * summed[t]
    else:
        for t in range(z.tiles):
            newres_ref[t] = summed[t]
    lane = iota((8, 128), 1)
    wide = up(z.nb, 128)

    def apply(g, carry):
        for p in range(z.per):
            slot = g * z.per + p
            acc = [jnp.zeros((8, z.nb), F32)] * 2
            for a in range(z.steps):
                block = inv_ref[slot, 8 * a : 8 * a + 8, :]
                for k in range(2):
                    col = newres_ref[k * z.groups + g][:, p * z.steps + a : p * z.steps + a + 1]
                    acc[k] = acc[k] + block * col
            live = iota((1, z.nb), 1) >= own_ref[slot]
            for k in range(2):
                value = jnp.where(live, jnp.sum(acc[k], axis=0, keepdims=True), 0.0)
                for c in range(wide // 128):
                    size = min(128, z.nb - c * 128)
                    flat[c, pl.ds(k * z.cnt + slot, 1), 0:size] = value[:, c * 128 : c * 128 + size]
        return carry

    flat[...] = jnp.zeros_like(flat)
    lax.fori_loop(0, z.groups, apply, 0)
    columns = jnp.concatenate([flat[c].T for c in range(wide // 128)], 0)
    energy = jnp.zeros((8, 128), F32)
    for g in range(z.groups):
        tiles = [jnp.zeros((8, 128), F32)] * 2
        for p in range(z.per):
            slot = g * z.per + p
            acc = [[jnp.zeros((8, 128), F32)] * z.halves for k in range(2)]
            for a in range(z.steps):
                f = [func_ref[h, slot * z.nb + 8 * a : slot * z.nb + 8 * a + 8, :] for h in range(z.halves)]
                for k in range(2):
                    r = k * z.cnt + slot
                    col = jnp.broadcast_to(columns[8 * a : 8 * a + 8, r : r + 1], (8, 128))
                    tiles[k] = jnp.where(lane == p * z.steps + a, col, tiles[k])
                    for h in range(z.halves):
                        acc[k][h] = acc[k][h] + f[h] * col
            for k in range(2):
                r = k * z.cnt + slot
                for h in range(z.halves):
                    out_ref[0, r : r + 1, h * 128 : (h + 1) * 128] = jnp.sum(acc[k][h], axis=0, keepdims=True)
        for k in range(2):
            t = k * z.groups + g
            prec_ref[t] = tiles[k]
            energy = energy + tiles[k] * newres_ref[t]
    rest = z.pay - 2 * z.cnt
    out_ref[0, 2 * z.cnt :, :] = jnp.broadcast_to(full_sum(energy), (rest, z.cyc))
    for d in range(1, z.nord):
        out_ref[d] = out_ref[0]


def make_step(z, own, gathered, inv, func, state=None):
    later = state is not None
    tile = jax.ShapeDtypeStruct((z.tiles, 8, 128), F32)
    outs = [jax.ShapeDtypeStruct((z.nord, z.pay, z.cyc), F32), tile, tile] + [tile] * later
    args = [own, gathered, inv, func] + (list(state) if later else [])
    return pl.pallas_call(
        functools.partial(step_kernel, z, later),
        in_specs=[SMEM] + [VMEM] * (len(args) - 1),
        out_specs=[VMEM] * len(outs),
        out_shape=outs,
        scratch_shapes=[pltpu.VMEM((up(z.nb, 128) // 128, up(2 * z.cnt, 8), 128), F32)],
        name="step",
    )(*args)


def image_kernel(z, later, own_ref, ids_ref, recv_ref, tc_ref, ts_ref, func_ref, *refs):
    if later:
        old_ref, old_energy_ref, prec_ref, old_dir_ref = refs[:4]
        out_ref, energy_ref, dir_ref, val_ref, all_rows, rows = refs[4:]
    else:
        out_ref, energy_ref, val_ref, all_rows, rows = refs
    energy = recv_ref[0, 2 * z.cnt : 2 * z.cnt + 1, 0:128]
    for o in range(1, z.nord):
        energy = energy + recv_ref[o, 2 * z.cnt : 2 * z.cnt + 1, 0:128]
    energy_ref[...] = jnp.broadcast_to(energy, (8, 128))

    def place(o, carry):
        for i in range(z.cnt):
            order = ids_ref[o * z.cnt + i]
            for k in range(2):
                for h in range(z.halves):
                    val_ref[k, h, pl.ds(order, 1), :] = recv_ref[o, k * z.cnt + i : k * z.cnt + i + 1, h * 128 : (h + 1) * 128]
        return carry

    lax.fori_loop(0, z.nord, place, 0)
    if later:
        ratio = energy / old_energy_ref[0:1, :]
        for k in range(2):
            for h in range(z.halves):
                val_ref[k, h] = val_ref[k, h] + ratio * old_ref[k, h]
        for t in range(z.tiles):
            dir_ref[t] = prec_ref[t] + ratio * old_dir_ref[t]

    def one_order(m, total):
        for h in range(z.halves):
            vc, vs = val_ref[0, h], val_ref[1, h]
            near, far = tc_ref[h, pl.ds(z.off - m, z.no), :], tc_ref[h, pl.ds(z.off + m, z.no), :]
            snear, sfar = ts_ref[h, pl.ds(z.off - m, z.no), :], ts_ref[h, pl.ds(z.off + m, z.no), :]
            wc = 0.5 * jnp.sum((near + far) * vc + (sfar + snear) * vs, axis=0, keepdims=True)
            ws = 0.5 * jnp.sum((sfar - snear) * vc + (near - far) * vs, axis=0, keepdims=True)
            all_rows[h, pl.ds(m, 1), :] = wc
            all_rows[z.halves + h, pl.ds(m, 1), :] = ws
        return total

    lax.fori_loop(0, z.no, one_order, 0)
    curvature = jnp.zeros((z.no, 128), F32)
    for k in range(2):
        for h in range(z.halves):
            curvature = curvature + all_rows[k * z.halves + h] * val_ref[k, h]
    for i in range(z.cnt):
        for k in range(2):
            for h in range(z.halves):
                rows[h, k * z.cnt + i : k * z.cnt + i + 1, :] = all_rows[
                    k * z.halves + h, pl.ds(own_ref[i], 1), :
                ]
    adjoint_into(z, func_ref, rows, out_ref)
    mark = (iota((8, 128), 1) == 127) & (iota((8, 128), 0) == 0)
    out_ref[0] = jnp.where(mark, full_sum(curvature), out_ref[0])


def make_image(z, own, ids, recv, tc, ts, func, state=None):
    later = state is not None
    tile = jax.ShapeDtypeStruct((z.tiles, 8, 128), F32)
    outs = [tile, jax.ShapeDtypeStruct((8, 128), F32)] + [tile] * later
    outs.append(jax.ShapeDtypeStruct((2, z.halves, z.no, 128), F32))
    args = [own, ids, recv, tc, ts, func] + (list(state) if later else [])
    return pl.pallas_call(
        functools.partial(image_kernel, z, later),
        in_specs=[SMEM, SMEM] + [VMEM] * (len(args) - 2),
        out_specs=[VMEM] * len(outs),
        out_shape=outs,
        scratch_shapes=[
            pltpu.VMEM((2 * z.halves, z.no, 128), F32),
            pltpu.VMEM((z.halves, z.pay, 128), F32),
        ],
        name="image",
    )(*args)


def last_kernel(z, gathered_ref, energy_ref, res_ref, sol_ref, dir_ref, out_sol, out_res):
    summed, curvature = total_of(z, gathered_ref)
    step_size = energy_ref[0:1, 0:1] / curvature
    lane = iota((8, 128), 1)
    finals = (
        [sol_ref[t] + step_size * dir_ref[t] for t in range(z.tiles)],
        [res_ref[t] - step_size * summed[t] for t in range(z.tiles)],
    )
    wide = up(z.nb, 128)
    for tiles, out in zip(finals, (out_sol, out_res)):
        columns = []
        for a in range(z.steps):
            tile = jnp.zeros((8, 128), F32)
            for slot in range(z.cnt):
                g, p = divmod(slot, z.per)
                for k in range(2):
                    col = tiles[k * z.groups + g][:, p * z.steps + a : p * z.steps + a + 1]
                    tile = jnp.where(lane == 2 * slot + k, col, tile)
            columns.append(tile)
        columns += [jnp.zeros((8, 128), F32)] * ((wide - z.nb) // 8)
        for c in range(wide // 128):
            flat = jnp.concatenate(columns[16 * c : 16 * c + 16], 0).T
            size = min(128, z.nb - c * 128)
            for slot in range(z.cnt):
                out[slot, :, c * 128 : c * 128 + size] = flat[2 * slot : 2 * slot + 2, 0:size]


def make_last(z, gathered, energy, res, sol, direction):
    out = jax.ShapeDtypeStruct((z.cnt, 2, z.nb), F32)
    return pl.pallas_call(
        functools.partial(last_kernel, z),
        in_specs=[VMEM] * 5,
        out_specs=[VMEM] * 2,
        out_shape=[out, out],
        name="last",
    )(gathered, energy, res, sol, direction)


def body(longitude, cycle_of, obs_count, observed, obs_weight, legendre, precond_inv, order_of_slot):
    z = Sizes(legendre, longitude.shape[1])
    dense = lambda value: value.reshape(z.rows, 128)
    first = (lax.axis_index("ord") * z.cnt).astype(jnp.int32).reshape(1)
    seeds = make_seeds(z, first, order_of_slot, legendre)
    recv = lax.all_to_all(seeds, "ord", 0, 0)
    tc, ts, ty = make_tables(
        z, obs_count, order_of_slot, dense(longitude), dense(cycle_of), dense(observed), dense(obs_weight)
    )
    ids = recv[:, z.id_row, : z.cnt].reshape(z.no).astype(jnp.int32)
    func, part = make_functions(z, order_of_slot, recv, ty)
    gathered = lax.all_gather(part, "obs", axis=0)
    values, res, direction = make_step(z, order_of_slot, gathered, precond_inv, func)
    recv = lax.all_to_all(values, "ord", 0, 0)
    part, energy, all_values = make_image(z, order_of_slot, ids, recv, tc, ts, func)
    gathered = lax.all_gather(part, "obs", axis=0)
    values, res, prec, sol = make_step(z, order_of_slot, gathered, precond_inv, func, (energy, res, direction))
    recv = lax.all_to_all(values, "ord", 0, 0)
    part, energy, direction, all_values = make_image(
        z, order_of_slot, ids, recv, tc, ts, func, (all_values, energy, prec, direction)
    )
    gathered = lax.all_gather(part, "obs", axis=0)
    return tuple(make_last(z, gathered, energy, res, sol, direction))


def solution(mesh):
    placed = (
        P("obs", None),
        P("obs", None),
        P("obs"),
        P("obs", None),
        P("obs", None),
        P("obs", "ord", None, None),
        P("ord", None, None),
        P("ord"),
    )
    return jax.shard_map(
        body,
        mesh=mesh,
        in_specs=placed,
        out_specs=(P("ord", None, None), P("ord", None, None)),
        check_vma=False,
    )
```

```python
import functools

import jax
import jax.numpy as jnp
from jax import lax
from jax.experimental import pallas as pl
from jax.experimental.pallas import tpu as pltpu
from jax.sharding import PartitionSpec as P

ITERS = 2
SEGMENTS = 2
VMEM_LIMIT = 24 << 20
WINDOW = 32
UNROLL = 4
CHUNK = 1024
F32 = jnp.float32
BF16 = jnp.bfloat16

VMEM = pl.BlockSpec(memory_space=pltpu.VMEM)
SMEM = pl.BlockSpec(memory_space=pltpu.SMEM)
HBM = pl.BlockSpec(memory_space=pltpu.MemorySpace.HBM)


def up(value, unit):
    return -(-value // unit) * unit


def iota(shape, axis):
    return lax.broadcasted_iota(jnp.int32, shape, axis)


class Sizes:
    def __init__(self, legendre, slab):
        self.cnt, self.nb, self.cyc = legendre.shape[1:]
        self.nord = lax.axis_size("ord")
        self.nobs = lax.axis_size("obs")
        self.no = self.cnt * self.nord
        self.slab = slab
        self.rows = slab // 128
        self.halves = self.cyc // 128
        self.steps = self.nb // 8
        per = 128 // self.steps
        while self.cnt % per or per * self.steps == 128:
            per -= 1
        self.per = per
        self.groups = self.cnt // per
        self.tiles = 2 * self.groups
        self.seg = SEGMENTS
        self.seg_len = self.nb // SEGMENTS
        self.seed_rows = 2 * self.seg + 1
        self.id_row = self.cnt * self.seed_rows
        self.seeds = up(self.id_row + 1, 8)
        self.pay = up(2 * self.cnt + 1, 8)
        self.off = up(self.no, 8)
        self.share = -(-(2 * self.no - 1) // self.nord)
        self.freq = self.share * self.nord
        self.table = up(self.off + self.freq, 8)
        self.sums = up(2 * (self.share + self.cnt), 16)
        self.pay_first = up(2 * self.cnt + 1 + 2 * self.share, 8)
        self.width = min(CHUNK // 128, self.rows)
        self.chunks = self.rows // self.width
        self.windows = self.cyc // WINDOW
        self.skew = self.rows + 1
        self.seg_skew = self.seg_len + 1
        self.func_rows = up(self.cnt * self.seg * self.seg_skew, 8)
        self.pairs = up(self.chunks + self.windows - 1, UNROLL)
        self.sum_lanes = up(2 * self.sums, 128)
        self.limit = VMEM_LIMIT

    def func_row(self, slot, a):
        segment, at = divmod(8 * a, self.seg_len)
        return (slot * self.seg + segment) * self.seg_skew + at


def send_copies(z, source, out_ref, sems):
    copies = [pltpu.make_async_copy(source, out_ref.at[d], sems.at[d]) for d in range(z.nord)]
    for copy in copies:
        copy.start()
    for copy in copies:
        copy.wait()


def seeds_kernel(z, first_ref, own_ref, leg_ref, out_ref, stage, keep, sems, out_sems):
    copies = []
    for i in range(z.cnt):
        aligned = pl.multiple_of((first_ref[0] + i) // 8 * 8, 8)
        for s in range(z.seg + 1):
            at = aligned if s == z.seg else s * z.seg_len
            n = i * (z.seg + 1) + s
            copies.append(pltpu.make_async_copy(leg_ref.at[0, i, pl.ds(at, 8), :], stage.at[n], sems.at[n]))
    for copy in copies:
        copy.start()
    lane = iota((z.seeds - z.id_row, z.cyc), 1)
    ids = jnp.zeros(lane.shape, F32)
    for slot in range(z.cnt):
        ids = jnp.where(lane == slot, own_ref[slot].astype(F32), ids)
    keep[z.id_row :, :] = ids
    for copy in copies:
        copy.wait()
    for i in range(z.cnt):
        base = i * z.seed_rows
        for s in range(z.seg):
            keep[base + 2 * s : base + 2 * s + 2, :] = stage[i * (z.seg + 1) + s, 0:2, :]
        order = first_ref[0] + i
        block = stage[i * (z.seg + 1) + z.seg]
        mine = iota((8, z.cyc), 0) == order - order // 8 * 8
        keep[base + 2 * z.seg : base + 2 * z.seg + 1, :] = jnp.sum(jnp.where(mine, block, 0.0), axis=0, keepdims=True)
    send_copies(z, keep, out_ref, out_sems)


def make_seeds(z, first, own, legendre):
    return pl.pallas_call(
        functools.partial(seeds_kernel, z),
        in_specs=[SMEM, SMEM, HBM],
        out_specs=HBM,
        out_shape=pltpu.MemorySpace.HBM((z.nord, z.seeds, z.cyc), F32),
        scratch_shapes=[
            pltpu.VMEM((z.cnt * (z.seg + 1), 8, z.cyc), F32),
            pltpu.VMEM((z.seeds, z.cyc), F32),
            pltpu.SemaphoreType.DMA((z.cnt * (z.seg + 1),)),
            pltpu.SemaphoreType.DMA((z.nord,)),
        ],
        compiler_params=pltpu.CompilerParams(vmem_limit_bytes=z.limit),
        name="seeds",
    )(first, own, legendre)


def sincos(angle):
    turn = jnp.round(angle * 0.6366197723675814)
    rest = angle - turn * 1.5703125
    rest = rest - turn * 4.837512969970703e-4
    rest = rest - turn * 7.549789948768648e-8
    sq = rest * rest
    sine = rest + rest * sq * (-0.16666654611 + sq * (8.3321608736e-3 + sq * -1.9515295891e-4))
    cosine = 1.0 - 0.5 * sq + sq * sq * (4.166664568298827e-2 + sq * (-1.388731625493765e-3 + sq * 2.443315711809948e-5))
    quarter = turn.astype(jnp.int32)
    odd = (quarter & 1) == 1
    c = jnp.where(odd, sine, cosine)
    s = jnp.where(odd, cosine, sine)
    c = jnp.where(((quarter + 1) & 2) == 2, -c, c)
    s = jnp.where((quarter & 2) == 2, -s, s)
    return c, s


def split(value):
    high = value.astype(BF16)
    return high, (value - high.astype(F32)).astype(BF16)


def tables_kernel(z, base_ref, count_ref, own_ref, lon_ref, cyc_ref, data_ref, weight_ref,
                  sum_ref, ty_ref, val, cyc_row, lhs, hot, acc, ids, pair_chunk, pair_window, sems):
    scalars = pltpu.make_async_copy(cyc_ref, ids, sems.at[0])
    scalars.start()
    total = z.slab * z.nobs
    size = min(32, z.rows)

    def block(i, carry):
        at = pl.multiple_of(i * size, 8)
        lon = lon_ref[pl.ds(at, size), :]
        place = at * 128 + iota((size, 128), 0) * 128 + iota((size, 128), 1)
        scale = weight_ref[pl.ds(at, size), :] * (place < count_ref[0]).astype(F32) / total
        c1, s1 = sincos(lon)
        c, s = sincos(base_ref[0].astype(F32) * lon)
        c, s = c * scale, s * scale
        for p in range(z.share):
            val[pl.ds(p * z.skew + at, size), :] = c
            val[pl.ds((z.share + p) * z.skew + at, size), :] = s
            c, s = c * c1 - s * s1, s * c1 + c * s1
        scaled = scale * data_ref[pl.ds(at, size), :]
        for slot in range(z.cnt):
            c, s = sincos(own_ref[slot].astype(F32) * lon)
            val[pl.ds((2 * z.share + slot) * z.skew + at, size), :] = c * scaled
            val[pl.ds((2 * z.share + z.cnt + slot) * z.skew + at, size), :] = s * scaled
        for row in range(2 * (z.share + z.cnt), z.sums):
            val[pl.ds(row * z.skew + at, size), :] = jnp.zeros((size, 128), F32)
        cyc_row[pl.ds(at, size), :] = cyc_ref[pl.ds(at, size), :].astype(F32)
        return carry

    lax.fori_loop(0, z.rows // size, block, 0)
    acc[...] = jnp.zeros_like(acc)
    width = z.width

    def fill(c, carry):
        for k in range(width):
            r = c * width + k
            lanes = slice(k * 128, (k + 1) * 128)
            for pair in range(z.sums // 16):
                first = val[pl.ds(pair * 16 * z.skew + r, 8, stride=z.skew), :]
                second = val[pl.ds((pair * 16 + 8) * z.skew + r, 8, stride=z.skew), :]
                high, low = split(jnp.concatenate([first, second], 0))
                lhs[c, pair * 16 : pair * 16 + 16, lanes] = high
                lhs[c, z.sums + pair * 16 : z.sums + pair * 16 + 16, lanes] = low
        return carry

    lax.fori_loop(0, z.chunks, fill, 0)
    scalars.wait()
    for n in range(z.pairs):
        pair_chunk[n] = 0
        pair_window[n] = z.windows

    def list_chunk(c, count):
        low = ids[c * width, 0] // WINDOW
        high = ids[c * width + width - 1, 127] // WINDOW

        def add(w, at):
            pair_chunk[at] = c
            pair_window[at] = w
            return at + 1

        return lax.fori_loop(low, high + 1, add, count)

    lax.fori_loop(0, z.chunks, list_chunk, 0)
    cycle_id = iota((WINDOW, 128), 0).astype(F32)

    def some(step, carry):
        for u in range(UNROLL):
            c = pair_chunk[step * UNROLL + u]
            w = pair_window[step * UNROLL + u]
            base = (w * WINDOW).astype(F32)
            for k in range(width):
                here = cyc_row[pl.ds(c * width + k, 1), :] - base
                hot[u, :, k * 128 : (k + 1) * 128] = jnp.where(cycle_id == here, 1.0, 0.0).astype(BF16)
            acc[w] += lax.dot_general(hot[u], lhs[c], (((1,), (1,)), ((), ())), preferred_element_type=F32)
        return carry

    lax.fori_loop(0, z.pairs // UNROLL, some, 0)
    both = 2 * z.share
    per_half = 128 // WINDOW
    for h in range(z.halves):
        flat = jnp.concatenate([acc[h * per_half + w] for w in range(per_half)], 0)
        flat = jnp.concatenate([flat[:, c * 128 : (c + 1) * 128].T for c in range(z.sum_lanes // 128)], 0)
        sum_ref[h, 0:both, :] = flat[0:both] + flat[z.sums : z.sums + both]
        ty_ref[h, 0 : 2 * z.cnt, :] = (
            flat[both : both + 2 * z.cnt] + flat[z.sums + both : z.sums + both + 2 * z.cnt]
        )


def make_tables(z, base, count, own, lon, cyc, data, weight):
    return pl.pallas_call(
        functools.partial(tables_kernel, z),
        in_specs=[SMEM, SMEM, SMEM] + [VMEM] * 4,
        out_specs=[VMEM] * 2,
        out_shape=[
            jax.ShapeDtypeStruct((z.halves, up(2 * z.share, 8), 128), F32),
            jax.ShapeDtypeStruct((z.halves, z.pay, 128), F32),
        ],
        scratch_shapes=[
            pltpu.VMEM((up(z.sums * z.skew, 8), 128), F32),
            pltpu.VMEM((z.rows, 128), F32),
            pltpu.VMEM((z.chunks, z.sum_lanes, z.width * 128), BF16),
            pltpu.VMEM((UNROLL, WINDOW, z.width * 128), BF16),
            pltpu.VMEM((z.windows + 1, WINDOW, z.sum_lanes), F32),
            pltpu.SMEM((z.rows, 128), jnp.int32),
            pltpu.SMEM((z.pairs,), jnp.int32),
            pltpu.SMEM((z.pairs,), jnp.int32),
            pltpu.SemaphoreType.DMA((1,)),
        ],
        compiler_params=pltpu.CompilerParams(vmem_limit_bytes=2 * z.limit),
        name="tables",
    )(base, count, own, lon, cyc, data, weight)


def adjoint_into(z, func_ref, rows_ref, out_ref):
    lane = iota((8, 128), 1)

    def group(g, carry):
        tiles = [jnp.zeros((8, 128), F32)] * 2
        for p in range(z.per):
            slot = g * z.per + p
            w = [
                [
                    jnp.broadcast_to(rows_ref[h, pl.ds(k * z.cnt + slot, 1), :], (8, 128))
                    for h in range(z.halves)
                ]
                for k in range(2)
            ]
            for a in range(z.steps):
                at = z.func_row(slot, a)
                f = [func_ref[h, pl.ds(at, 8), :] for h in range(z.halves)]
                for k in range(2):
                    prod = f[0] * w[k][0]
                    for h in range(1, z.halves):
                        prod = prod + f[h] * w[k][h]
                    tiles[k] = jnp.where(lane == p * z.steps + a, jnp.sum(prod, axis=1, keepdims=True), tiles[k])
        for k in range(2):
            out_ref[k * z.groups + g] = tiles[k]
        return carry

    lax.fori_loop(0, z.groups, group, 0)


def functions_kernel(z, own_ref, recv_ref, ty_ref, func_ref, out_ref, seed0, seed1, first):
    total = z.seg * z.cnt
    padded = up(total, 8)
    for slot in range(z.cnt):
        order = own_ref[slot]
        block = order // z.cnt
        base = (order - block * z.cnt) * z.seed_rows
        for s in range(z.seg):
            r = slot * z.seg + s
            seed0[r : r + 1, :] = recv_ref[block, pl.ds(base + 2 * s, 1), :]
            seed1[r : r + 1, :] = recv_ref[block, pl.ds(base + 2 * s + 1, 1), :]
            first[r : r + 1, :] = recv_ref[block, pl.ds(base + 2 * z.seg, 1), :]
    cosine = recv_ref[0, 1:2, :] / (recv_ref[0, 0:1, :] * 1.7320508075688772)
    lanes_len = up(z.seg_len, 128)
    row = iota((padded, lanes_len), 0)
    order_of = jnp.zeros(row.shape, F32)
    degree = jnp.zeros(row.shape, F32) + iota(row.shape, 1).astype(F32)
    for slot in range(z.cnt):
        for s in range(z.seg):
            hit = row == slot * z.seg + s
            order_of = jnp.where(hit, own_ref[slot].astype(F32), order_of)
            degree = jnp.where(hit, degree + float(s * z.seg_len), degree)
    minus = jnp.maximum(degree - order_of, 1.0)
    plus = jnp.maximum(degree + order_of, 1.0)
    rise = jnp.sqrt(jnp.maximum((2.0 * degree - 1.0) * (2.0 * degree + 1.0), 0.0) / (minus * plus))
    rise = jnp.where(degree > order_of, rise, 0.0)
    top = jnp.maximum((2.0 * degree + 1.0) * (degree + order_of - 1.0) * (degree - order_of - 1.0), 0.0)
    fall = jnp.sqrt(top / (minus * plus * jnp.maximum(2.0 * degree - 3.0, 1.0)))
    fall = jnp.where(degree > order_of + 1.0, fall, 0.0)
    starts = (degree == order_of).astype(F32)
    for h in range(z.halves):
        lanes = slice(h * 128, (h + 1) * 128)
        x = jnp.broadcast_to(cosine[:, lanes], (8, 128))
        for tile in range(padded // 8):
            rows = slice(tile * 8, tile * 8 + 8)
            left = min(8, total - tile * 8)
            before, prev = None, None
            for t in range(z.seg_len):
                if t == 0:
                    now = seed0[rows, lanes]
                elif t == 1:
                    now = seed1[rows, lanes]
                else:
                    now = (rise[rows, t : t + 1] * x) * prev - fall[rows, t : t + 1] * before
                    now = jnp.where(starts[rows, t : t + 1] > 0.5, first[rows, lanes], now)
                func_ref[h, pl.ds(tile * 8 * z.seg_skew + t, left, stride=z.seg_skew), :] = now[:left]
                before, prev = prev, now
    adjoint_into(z, func_ref, ty_ref, out_ref)


def make_functions(z, own, recv, ty):
    padded = up(z.seg * z.cnt, 8)
    return pl.pallas_call(
        functools.partial(functions_kernel, z),
        in_specs=[SMEM, VMEM, VMEM],
        out_specs=[VMEM] * 2,
        out_shape=[
            jax.ShapeDtypeStruct((z.halves, z.func_rows, 128), F32),
            jax.ShapeDtypeStruct((z.tiles, 8, 128), F32),
        ],
        scratch_shapes=[pltpu.VMEM((padded, z.cyc), F32)] * 3,
        compiler_params=pltpu.CompilerParams(vmem_limit_bytes=z.limit),
        name="functions",
    )(own, recv, ty)


def total_of(z, gathered_ref):
    summed = [gathered_ref[0, t] for t in range(z.tiles)]
    for b in range(1, z.nobs):
        summed = [summed[t] + gathered_ref[b, t] for t in range(z.tiles)]
    lane = iota((8, 128), 1)
    curvature = jnp.max(jnp.where((lane == 127) & (iota((8, 128), 0) == 0), summed[0], -jnp.inf), axis=1, keepdims=True)
    curvature = jnp.max(curvature, axis=0, keepdims=True)
    used = lane < z.per * z.steps
    return [jnp.where(used, s, 0.0) for s in summed], curvature


def full_sum(value):
    return jnp.sum(jnp.sum(value, axis=1, keepdims=True), axis=0, keepdims=True)


def step_kernel(z, later, own_ref, *refs):
    if later:
        gathered_ref, inv_ref, func_ref, energy_ref, res_ref, dir_ref = refs[:6]
        out_ref, newres_ref, prec_ref, sol_ref, flat, pay, inv_buf, sems, inv_sems = refs[6:]
    else:
        gathered_ref, inv_ref, func_ref, sum_ref = refs[:4]
        out_ref, newres_ref, prec_ref, flat, pay, inv_buf, sems, inv_sems = refs[4:]
    fetches = [pltpu.make_async_copy(inv_ref.at[slot], inv_buf.at[slot], inv_sems.at[slot]) for slot in range(z.cnt)]
    for fetch in fetches:
        fetch.start()
    summed, curvature = total_of(z, gathered_ref)
    if later:
        step_size = energy_ref[0:1, 0:1] / curvature
        for t in range(z.tiles):
            sol_ref[t] = step_size * dir_ref[t]
            newres_ref[t] = res_ref[t] - step_size * summed[t]
    else:
        for t in range(z.tiles):
            newres_ref[t] = summed[t]
    lane = iota((8, 128), 1)
    wide = up(z.nb, 128)

    def apply(g, carry):
        for p in range(z.per):
            slot = g * z.per + p
            pltpu.make_async_copy(inv_ref.at[slot], inv_buf.at[slot], inv_sems.at[slot]).wait()
            acc = [jnp.zeros((8, z.nb), F32)] * 2
            for a in range(z.steps):
                block = inv_buf[slot, 8 * a : 8 * a + 8, :]
                for k in range(2):
                    col = newres_ref[k * z.groups + g][:, p * z.steps + a : p * z.steps + a + 1]
                    acc[k] = acc[k] + block * col
            live = iota((1, z.nb), 1) >= own_ref[slot]
            for k in range(2):
                value = jnp.where(live, jnp.sum(acc[k], axis=0, keepdims=True), 0.0)
                for c in range(wide // 128):
                    size = min(128, z.nb - c * 128)
                    flat[c, pl.ds(k * z.cnt + slot, 1), 0:size] = value[:, c * 128 : c * 128 + size]
        return carry

    flat[...] = jnp.zeros_like(flat)
    lax.fori_loop(0, z.groups, apply, 0)
    columns = jnp.concatenate([flat[c].T for c in range(wide // 128)], 0)
    energy = jnp.zeros((8, 128), F32)
    for g in range(z.groups):
        tiles = [jnp.zeros((8, 128), F32)] * 2
        for p in range(z.per):
            slot = g * z.per + p
            acc = [[jnp.zeros((8, 128), F32)] * z.halves for k in range(2)]
            for a in range(z.steps):
                f = [func_ref[h, pl.ds(z.func_row(slot, a), 8), :] for h in range(z.halves)]
                for k in range(2):
                    r = k * z.cnt + slot
                    col = jnp.broadcast_to(columns[8 * a : 8 * a + 8, r : r + 1], (8, 128))
                    tiles[k] = jnp.where(lane == p * z.steps + a, col, tiles[k])
                    for h in range(z.halves):
                        acc[k][h] = acc[k][h] + f[h] * col
            for k in range(2):
                r = k * z.cnt + slot
                for h in range(z.halves):
                    pay[r : r + 1, h * 128 : (h + 1) * 128] = jnp.sum(acc[k][h], axis=0, keepdims=True)
        for k in range(2):
            t = k * z.groups + g
            prec_ref[t] = tiles[k]
            energy = energy + tiles[k] * newres_ref[t]
    top = 2 * z.cnt + 1
    pay[2 * z.cnt : top, :] = jnp.broadcast_to(full_sum(energy), (1, z.cyc))
    if not later:
        for h in range(z.halves):
            pay[top : top + 2 * z.share, h * 128 : (h + 1) * 128] = sum_ref[h, 0 : 2 * z.share, :]
    send_copies(z, pay, out_ref, sems)


def make_step(z, own, gathered, inv, func, state, later):
    tile = jax.ShapeDtypeStruct((z.tiles, 8, 128), F32)
    outs = [pltpu.MemorySpace.HBM((z.nord, z.pay if later else z.pay_first, z.cyc), F32), tile, tile] + [tile] * later
    args = [own, gathered, inv, func] + list(state)
    return pl.pallas_call(
        functools.partial(step_kernel, z, later),
        in_specs=[SMEM, VMEM, HBM] + [VMEM] * (len(args) - 3),
        out_specs=[HBM] + [VMEM] * (len(outs) - 1),
        out_shape=outs,
        scratch_shapes=[
            pltpu.VMEM((up(z.nb, 128) // 128, up(2 * z.cnt, 8), 128), F32),
            pltpu.VMEM(outs[0].shape[1:], F32),
            pltpu.VMEM(inv.shape, F32),
            pltpu.SemaphoreType.DMA((z.nord,)),
            pltpu.SemaphoreType.DMA((z.cnt,)),
        ],
        compiler_params=pltpu.CompilerParams(vmem_limit_bytes=z.limit),
        name="step",
    )(*args)


def image_kernel(z, later, own_ref, ids_ref, recv_ref, func_ref, *refs):
    if later:
        tc_ref, ts_ref, old_ref, old_energy_ref, prec_ref, old_dir_ref = refs[:6]
        out_ref, energy_ref, dir_ref, val_ref, all_rows, rows = refs[6:]
    else:
        out_ref, energy_ref, tc_ref, ts_ref, val_ref, all_rows, rows = refs
        top = 2 * z.cnt + 1
        for o in range(z.nord):
            at = z.off + o * z.share
            for h in range(z.halves):
                lanes = slice(h * 128, (h + 1) * 128)
                tc_ref[h, at : at + z.share, :] = recv_ref[o, top : top + z.share, lanes]
                ts_ref[h, at : at + z.share, :] = recv_ref[o, top + z.share : top + 2 * z.share, lanes]

        def mirror(q, carry):
            for h in range(z.halves):
                tc_ref[h, pl.ds(z.off - q, 1), :] = tc_ref[h, pl.ds(z.off + q, 1), :]
                ts_ref[h, pl.ds(z.off - q, 1), :] = -ts_ref[h, pl.ds(z.off + q, 1), :]
            return carry

        lax.fori_loop(1, z.no, mirror, 0)
    energy = recv_ref[0, 2 * z.cnt : 2 * z.cnt + 1, 0:128]
    for o in range(1, z.nord):
        energy = energy + recv_ref[o, 2 * z.cnt : 2 * z.cnt + 1, 0:128]
    energy_ref[...] = jnp.broadcast_to(energy, (8, 128))

    def place(o, carry):
        for i in range(z.cnt):
            order = ids_ref[o * z.cnt + i]
            for k in range(2):
                for h in range(z.halves):
                    val_ref[k, h, pl.ds(order, 1), :] = recv_ref[o, k * z.cnt + i : k * z.cnt + i + 1, h * 128 : (h + 1) * 128]
        return carry

    lax.fori_loop(0, z.nord, place, 0)
    if later:
        ratio = energy / old_energy_ref[0:1, :]
        for k in range(2):
            for h in range(z.halves):
                val_ref[k, h] = val_ref[k, h] + ratio * old_ref[k, h]
        for t in range(z.tiles):
            dir_ref[t] = prec_ref[t] + ratio * old_dir_ref[t]

    def one_order(m, total):
        for h in range(z.halves):
            vc, vs = val_ref[0, h], val_ref[1, h]
            near, far = tc_ref[h, pl.ds(z.off - m, z.no), :], tc_ref[h, pl.ds(z.off + m, z.no), :]
            snear, sfar = ts_ref[h, pl.ds(z.off - m, z.no), :], ts_ref[h, pl.ds(z.off + m, z.no), :]
            wc = 0.5 * jnp.sum((near + far) * vc + (sfar + snear) * vs, axis=0, keepdims=True)
            ws = 0.5 * jnp.sum((sfar - snear) * vc + (near - far) * vs, axis=0, keepdims=True)
            all_rows[h, pl.ds(m, 1), :] = wc
            all_rows[z.halves + h, pl.ds(m, 1), :] = ws
        return total

    lax.fori_loop(0, z.no, one_order, 0)
    curvature = jnp.zeros((z.no, 128), F32)
    for k in range(2):
        for h in range(z.halves):
            curvature = curvature + all_rows[k * z.halves + h] * val_ref[k, h]
    for i in range(z.cnt):
        for k in range(2):
            for h in range(z.halves):
                rows[h, k * z.cnt + i : k * z.cnt + i + 1, :] = all_rows[
                    k * z.halves + h, pl.ds(own_ref[i], 1), :
                ]
    adjoint_into(z, func_ref, rows, out_ref)
    mark = (iota((8, 128), 1) == 127) & (iota((8, 128), 0) == 0)
    out_ref[0] = jnp.where(mark, full_sum(curvature), out_ref[0])


def make_image(z, own, ids, recv, func, state=()):
    later = len(state) > 0
    tile = jax.ShapeDtypeStruct((z.tiles, 8, 128), F32)
    table = jax.ShapeDtypeStruct((z.halves, z.table, 128), F32)
    outs = [tile, jax.ShapeDtypeStruct((8, 128), F32)] + ([tile] if later else [table, table])
    outs.append(jax.ShapeDtypeStruct((2, z.halves, z.no, 128), F32))
    args = [own, ids, recv, func] + list(state)
    return pl.pallas_call(
        functools.partial(image_kernel, z, later),
        in_specs=[SMEM, SMEM] + [VMEM] * (len(args) - 2),
        out_specs=[VMEM] * len(outs),
        out_shape=outs,
        scratch_shapes=[
            pltpu.VMEM((2 * z.halves, z.no, 128), F32),
            pltpu.VMEM((z.halves, z.pay, 128), F32),
        ],
        compiler_params=pltpu.CompilerParams(vmem_limit_bytes=z.limit),
        name="image",
    )(*args)


def last_kernel(z, gathered_ref, energy_ref, res_ref, sol_ref, dir_ref, out_sol, out_res):
    summed, curvature = total_of(z, gathered_ref)
    step_size = energy_ref[0:1, 0:1] / curvature
    lane = iota((8, 128), 1)
    finals = (
        [sol_ref[t] + step_size * dir_ref[t] for t in range(z.tiles)],
        [res_ref[t] - step_size * summed[t] for t in range(z.tiles)],
    )
    wide = up(z.nb, 128)
    for tiles, out in zip(finals, (out_sol, out_res)):
        columns = []
        for a in range(z.steps):
            tile = jnp.zeros((8, 128), F32)
            for slot in range(z.cnt):
                g, p = divmod(slot, z.per)
                for k in range(2):
                    col = tiles[k * z.groups + g][:, p * z.steps + a : p * z.steps + a + 1]
                    tile = jnp.where(lane == 2 * slot + k, col, tile)
            columns.append(tile)
        columns += [jnp.zeros((8, 128), F32)] * ((wide - z.nb) // 8)
        for c in range(wide // 128):
            flat = jnp.concatenate(columns[16 * c : 16 * c + 16], 0).T
            size = min(128, z.nb - c * 128)
            for slot in range(z.cnt):
                out[slot, :, c * 128 : c * 128 + size] = flat[2 * slot : 2 * slot + 2, 0:size]


def make_last(z, gathered, energy, res, sol, direction):
    out = jax.ShapeDtypeStruct((z.cnt, 2, z.nb), F32)
    return pl.pallas_call(
        functools.partial(last_kernel, z),
        in_specs=[VMEM] * 5,
        out_specs=[VMEM] * 2,
        out_shape=[out, out],
        compiler_params=pltpu.CompilerParams(vmem_limit_bytes=z.limit),
        name="last",
    )(gathered, energy, res, sol, direction)


def body(longitude, cycle_of, obs_count, observed, obs_weight, legendre, precond_inv, order_of_slot):
    z = Sizes(legendre, longitude.shape[1])
    dense = lambda value: value.reshape(z.rows, 128)
    legendre = pltpu.with_memory_space_constraint(legendre, pltpu.MemorySpace.HBM)
    inv = pltpu.with_memory_space_constraint(precond_inv, pltpu.MemorySpace.HBM)
    first = (lax.axis_index("ord") * z.cnt).astype(jnp.int32).reshape(1)
    seeds = make_seeds(z, first, order_of_slot, legendre)
    recv = lax.all_to_all(seeds, "ord", 0, 0)
    base = (lax.axis_index("ord") * z.share).astype(jnp.int32).reshape(1)
    sums, ty = make_tables(
        z, base, obs_count, order_of_slot, dense(longitude), dense(cycle_of), dense(observed), dense(obs_weight)
    )
    ids = recv[:, z.id_row, : z.cnt].reshape(z.no).astype(jnp.int32)
    func, part = make_functions(z, order_of_slot, recv, ty)
    gathered = lax.all_gather(part, "obs", axis=0)
    values, res, direction = make_step(z, order_of_slot, gathered, inv, func, (sums,), False)
    recv = lax.all_to_all(values, "ord", 0, 0)
    part, energy, tc, ts, all_values = make_image(z, order_of_slot, ids, recv, func)
    gathered = lax.all_gather(part, "obs", axis=0)
    values, res, prec, sol = make_step(z, order_of_slot, gathered, inv, func, (energy, res, direction), True)
    recv = lax.all_to_all(values, "ord", 0, 0)
    part, energy, direction, all_values = make_image(
        z, order_of_slot, ids, recv, func, (tc, ts, all_values, energy, prec, direction)
    )
    gathered = lax.all_gather(part, "obs", axis=0)
    return tuple(make_last(z, gathered, energy, res, sol, direction))


def solution(mesh):
    placed = (
        P("obs", None),
        P("obs", None),
        P("obs"),
        P("obs", None),
        P("obs", None),
        P("obs", "ord", None, None),
        P("ord", None, None),
        P("ord"),
    )
    return jax.shard_map(
        body,
        mesh=mesh,
        in_specs=placed,
        out_specs=(P("ord", None, None), P("ord", None, None)),
        check_vma=False,
    )
```

```python
import functools

import jax
import jax.numpy as jnp
from jax import lax
from jax.experimental import pallas as pl
from jax.experimental.pallas import tpu as pltpu
from jax.sharding import PartitionSpec as P

ITERS = 2
SEGMENTS = 2
VMEM_LIMIT = 24 << 20
WINDOW = 32
UNROLL = 4
ORDERS_AT_ONCE = 2
CHUNK = 1024
F32 = jnp.float32
BF16 = jnp.bfloat16

VMEM = pl.BlockSpec(memory_space=pltpu.VMEM)
SMEM = pl.BlockSpec(memory_space=pltpu.SMEM)
HBM = pl.BlockSpec(memory_space=pltpu.MemorySpace.HBM)


def up(value, unit):
    return -(-value // unit) * unit


def iota(shape, axis):
    return lax.broadcasted_iota(jnp.int32, shape, axis)


class Sizes:
    def __init__(self, legendre, slab):
        self.cnt, self.nb, self.cyc = legendre.shape[1:]
        self.nord = lax.axis_size("ord")
        self.nobs = lax.axis_size("obs")
        self.no = self.cnt * self.nord
        self.slab = slab
        self.rows = slab // 128
        self.halves = self.cyc // 128
        self.steps = self.nb // 8
        self.state = (up(2 * self.cnt + 1, 8), up(self.nb, 128))
        self.seg = SEGMENTS
        self.seg_len = self.nb // SEGMENTS
        self.seed_rows = 2 * self.seg - 1
        self.cos_row = self.cnt * self.seed_rows
        self.id_row = self.cos_row + 1
        self.seeds = up(self.id_row + 1, 8)
        self.pay = up(2 * self.cnt + 1, 8)
        self.off = up(self.no, 8)
        self.share = -(-(2 * self.no - 1) // self.nord)
        self.freq = self.share * self.nord
        self.table = up(self.off + self.freq, 8)
        self.sums = up(2 * (self.share + self.cnt), 16)
        self.pay_first = up(2 * self.cnt + 1 + 2 * self.share, 8)
        self.width = min(CHUNK // 128, self.rows)
        self.chunks = self.rows // self.width
        self.windows = self.cyc // WINDOW
        self.skew = self.rows + 1
        self.seg_skew = self.seg_len + 1
        self.func_rows = up(self.cnt * self.seg * self.seg_skew, 8)
        self.pairs = up(self.chunks + self.windows - 1, UNROLL)
        self.sum_lanes = up(2 * self.sums, 128)
        self.limit = VMEM_LIMIT

    def func_row(self, slot, a):
        segment, at = divmod(8 * a, self.seg_len)
        return (slot * self.seg + segment) * self.seg_skew + at


def send_copies(z, source, out_ref, sems):
    copies = [pltpu.make_async_copy(source, out_ref.at[d], sems.at[d]) for d in range(z.nord)]
    for copy in copies:
        copy.start()
    for copy in copies:
        copy.wait()


def seeds_kernel(z, first_ref, own_ref, leg_ref, out_ref, stage, keep, sems, out_sems):
    copies = []

    def fetch(i, at):
        n = len(copies)
        copies.append(pltpu.make_async_copy(leg_ref.at[0, i, pl.ds(at, 8), :], stage.at[n], sems.at[n]))

    for i in range(z.cnt):
        for s in range(1, z.seg):
            fetch(i, s * z.seg_len)
        fetch(i, pl.multiple_of((first_ref[0] + i) // 8 * 8, 8))
    fetch(0, 0)
    for copy in copies:
        copy.start()
    lane = iota((z.seeds - z.id_row, z.cyc), 1)
    ids = jnp.zeros(lane.shape, F32)
    for slot in range(z.cnt):
        ids = jnp.where(lane == slot, own_ref[slot].astype(F32), ids)
    keep[z.id_row :, :] = ids
    for copy in copies:
        copy.wait()
    for i in range(z.cnt):
        base = i * z.seed_rows
        for s in range(z.seg - 1):
            keep[base + 2 * s : base + 2 * s + 2, :] = stage[i * z.seg + s, 0:2, :]
        order = first_ref[0] + i
        block = stage[i * z.seg + z.seg - 1]
        mine = iota((8, z.cyc), 0) == order - order // 8 * 8
        top = base + z.seed_rows - 1
        keep[top : top + 1, :] = jnp.sum(jnp.where(mine, block, 0.0), axis=0, keepdims=True)
    keep[z.cos_row : z.cos_row + 1, :] = stage[z.cnt * z.seg, 1:2, :]
    send_copies(z, keep, out_ref, out_sems)


def make_seeds(z, first, own, legendre):
    slabs = z.cnt * z.seg + 1
    return pl.pallas_call(
        functools.partial(seeds_kernel, z),
        in_specs=[SMEM, SMEM, HBM],
        out_specs=HBM,
        out_shape=pltpu.MemorySpace.HBM((z.nord, z.seeds, z.cyc), F32),
        scratch_shapes=[
            pltpu.VMEM((slabs, 8, z.cyc), F32),
            pltpu.VMEM((z.seeds, z.cyc), F32),
            pltpu.SemaphoreType.DMA((slabs,)),
            pltpu.SemaphoreType.DMA((z.nord,)),
        ],
        compiler_params=pltpu.CompilerParams(vmem_limit_bytes=z.limit),
        name="seeds",
    )(first, own, legendre)


def sincos(angle):
    turn = jnp.round(angle * 0.6366197723675814)
    rest = angle - turn * 1.5703125
    rest = rest - turn * 4.837512969970703e-4
    rest = rest - turn * 7.549789948768648e-8
    sq = rest * rest
    sine = rest + rest * sq * (-0.16666654611 + sq * (8.3321608736e-3 + sq * -1.9515295891e-4))
    cosine = 1.0 - 0.5 * sq + sq * sq * (4.166664568298827e-2 + sq * (-1.388731625493765e-3 + sq * 2.443315711809948e-5))
    quarter = turn.astype(jnp.int32)
    odd = (quarter & 1) == 1
    c = jnp.where(odd, sine, cosine)
    s = jnp.where(odd, cosine, sine)
    c = jnp.where(((quarter + 1) & 2) == 2, -c, c)
    s = jnp.where((quarter & 2) == 2, -s, s)
    return c, s


def split(value):
    high = value.astype(BF16)
    return high, (value - high.astype(F32)).astype(BF16)


def tables_kernel(z, base_ref, count_ref, own_ref, lon_ref, cyc_ref, data_ref, weight_ref,
                  sum_ref, ty_ref, val, cyc_row, lhs, hot, acc, ids, pair_chunk, pair_window, sems):
    scalars = pltpu.make_async_copy(cyc_ref, ids, sems.at[0])
    scalars.start()
    total = z.slab * z.nobs
    size = min(32, z.rows)

    def block(i, carry):
        at = pl.multiple_of(i * size, 8)
        lon = lon_ref[pl.ds(at, size), :]
        place = at * 128 + iota((size, 128), 0) * 128 + iota((size, 128), 1)
        scale = weight_ref[pl.ds(at, size), :] * (place < count_ref[0]).astype(F32) / total
        c1, s1 = sincos(lon)
        c, s = sincos(base_ref[0].astype(F32) * lon)
        c, s = c * scale, s * scale
        for p in range(z.share):
            val[pl.ds(p * z.skew + at, size), :] = c
            val[pl.ds((z.share + p) * z.skew + at, size), :] = s
            c, s = c * c1 - s * s1, s * c1 + c * s1
        scaled = scale * data_ref[pl.ds(at, size), :]
        for slot in range(z.cnt):
            c, s = sincos(own_ref[slot].astype(F32) * lon)
            val[pl.ds((2 * z.share + slot) * z.skew + at, size), :] = c * scaled
            val[pl.ds((2 * z.share + z.cnt + slot) * z.skew + at, size), :] = s * scaled
        for row in range(2 * (z.share + z.cnt), z.sums):
            val[pl.ds(row * z.skew + at, size), :] = jnp.zeros((size, 128), F32)
        cyc_row[pl.ds(at, size), :] = cyc_ref[pl.ds(at, size), :].astype(F32)
        return carry

    lax.fori_loop(0, z.rows // size, block, 0)
    acc[...] = jnp.zeros_like(acc)
    width = z.width

    def fill(c, carry):
        for k in range(width):
            r = c * width + k
            lanes = slice(k * 128, (k + 1) * 128)
            for pair in range(z.sums // 16):
                first = val[pl.ds(pair * 16 * z.skew + r, 8, stride=z.skew), :]
                second = val[pl.ds((pair * 16 + 8) * z.skew + r, 8, stride=z.skew), :]
                high, low = split(jnp.concatenate([first, second], 0))
                lhs[c, pair * 16 : pair * 16 + 16, lanes] = high
                lhs[c, z.sums + pair * 16 : z.sums + pair * 16 + 16, lanes] = low
        return carry

    lax.fori_loop(0, z.chunks, fill, 0)
    scalars.wait()
    for n in range(z.pairs):
        pair_chunk[n] = 0
        pair_window[n] = z.windows

    def list_chunk(c, count):
        low = ids[c * width, 0] // WINDOW
        high = ids[c * width + width - 1, 127] // WINDOW

        def add(w, at):
            pair_chunk[at] = c
            pair_window[at] = w
            return at + 1

        return lax.fori_loop(low, high + 1, add, count)

    lax.fori_loop(0, z.chunks, list_chunk, 0)
    cycle_id = iota((WINDOW, 128), 0).astype(F32)

    def some(step, carry):
        for u in range(UNROLL):
            c = pair_chunk[step * UNROLL + u]
            w = pair_window[step * UNROLL + u]
            base = (w * WINDOW).astype(F32)
            for k in range(width):
                here = cyc_row[pl.ds(c * width + k, 1), :] - base
                hot[u, :, k * 128 : (k + 1) * 128] = jnp.where(cycle_id == here, 1.0, 0.0).astype(BF16)
            acc[w] += lax.dot_general(hot[u], lhs[c], (((1,), (1,)), ((), ())), preferred_element_type=F32)
        return carry

    lax.fori_loop(0, z.pairs // UNROLL, some, 0)
    both = 2 * z.share
    per_half = 128 // WINDOW
    for h in range(z.halves):
        flat = jnp.concatenate([acc[h * per_half + w] for w in range(per_half)], 0)
        flat = jnp.concatenate([flat[:, c * 128 : (c + 1) * 128].T for c in range(z.sum_lanes // 128)], 0)
        sum_ref[h, 0:both, :] = flat[0:both] + flat[z.sums : z.sums + both]
        ty_ref[h, 0 : 2 * z.cnt, :] = (
            flat[both : both + 2 * z.cnt] + flat[z.sums + both : z.sums + both + 2 * z.cnt]
        )


def make_tables(z, base, count, own, lon, cyc, data, weight):
    return pl.pallas_call(
        functools.partial(tables_kernel, z),
        in_specs=[SMEM, SMEM, SMEM] + [VMEM] * 4,
        out_specs=[VMEM] * 2,
        out_shape=[
            jax.ShapeDtypeStruct((z.halves, up(2 * z.share, 8), 128), F32),
            jax.ShapeDtypeStruct((z.halves, z.pay, 128), F32),
        ],
        scratch_shapes=[
            pltpu.VMEM((up(z.sums * z.skew, 8), 128), F32),
            pltpu.VMEM((z.rows, 128), F32),
            pltpu.VMEM((z.chunks, z.sum_lanes, z.width * 128), BF16),
            pltpu.VMEM((UNROLL, WINDOW, z.width * 128), BF16),
            pltpu.VMEM((z.windows + 1, WINDOW, z.sum_lanes), F32),
            pltpu.SMEM((z.rows, 128), jnp.int32),
            pltpu.SMEM((z.pairs,), jnp.int32),
            pltpu.SMEM((z.pairs,), jnp.int32),
            pltpu.SemaphoreType.DMA((1,)),
        ],
        compiler_params=pltpu.CompilerParams(vmem_limit_bytes=2 * z.limit),
        name="tables",
    )(base, count, own, lon, cyc, data, weight)


def flip(z, cols_ref, out_ref):
    for c in range(z.state[1] // 128):
        out_ref[:, c * 128 : (c + 1) * 128] = cols_ref[c * 128 : (c + 1) * 128, :].T[0 : z.state[0]]


def adjoint_into(z, func_ref, rows_ref, cols_ref, out_ref):
    cols_ref[...] = jnp.zeros_like(cols_ref)
    for slot in range(z.cnt):
        w = [
            [
                jnp.broadcast_to(rows_ref[h, k * z.cnt + slot : k * z.cnt + slot + 1, :], (8, 128))
                for h in range(z.halves)
            ]
            for k in range(2)
        ]
        for a in range(z.steps):
            f = [func_ref[h, pl.ds(z.func_row(slot, a), 8), :] for h in range(z.halves)]
            for k in range(2):
                prod = f[0] * w[k][0]
                for h in range(1, z.halves):
                    prod = prod + f[h] * w[k][h]
                r = k * z.cnt + slot
                cols_ref[8 * a : 8 * a + 8, r : r + 1] = jnp.sum(prod, axis=1, keepdims=True)
    flip(z, cols_ref, out_ref)


def functions_kernel(z, own_ref, recv_ref, ty_ref, func_ref, out_ref, seed0, seed1, first, cols):
    total = z.seg * z.cnt
    padded = up(total, 8)
    for slot in range(z.cnt):
        order = own_ref[slot]
        block = order // z.cnt
        base = (order - block * z.cnt) * z.seed_rows
        for s in range(z.seg):
            r = slot * z.seg + s
            if s > 0:
                seed0[r : r + 1, :] = recv_ref[block, pl.ds(base + 2 * s - 2, 1), :]
                seed1[r : r + 1, :] = recv_ref[block, pl.ds(base + 2 * s - 1, 1), :]
            else:
                seed0[r : r + 1, :] = jnp.zeros((1, z.cyc), F32)
                seed1[r : r + 1, :] = jnp.zeros((1, z.cyc), F32)
            first[r : r + 1, :] = recv_ref[block, pl.ds(base + z.seed_rows - 1, 1), :]
    ground = recv_ref[0, z.seed_rows - 1 : z.seed_rows, :]
    cosine = recv_ref[0, z.cos_row : z.cos_row + 1, :] / (ground * 1.7320508075688772)
    lanes_len = up(z.seg_len, 128)
    row = iota((padded, lanes_len), 0)
    order_of = jnp.zeros(row.shape, F32)
    start_of = jnp.zeros(row.shape, F32)
    for slot in range(z.cnt):
        for s in range(z.seg):
            hit = row == slot * z.seg + s
            order_of = jnp.where(hit, own_ref[slot].astype(F32), order_of)
            start_of = jnp.where(hit, float(s * z.seg_len), start_of)
    degree = start_of + iota(row.shape, 1).astype(F32)
    minus = jnp.maximum(degree - order_of, 1.0)
    plus = jnp.maximum(degree + order_of, 1.0)
    rise = jnp.sqrt(jnp.maximum((2.0 * degree - 1.0) * (2.0 * degree + 1.0), 0.0) / (minus * plus))
    rise = jnp.where(degree > order_of, rise, 0.0)
    top = jnp.maximum((2.0 * degree + 1.0) * (degree + order_of - 1.0) * (degree - order_of - 1.0), 0.0)
    fall = jnp.sqrt(top / (minus * plus * jnp.maximum(2.0 * degree - 3.0, 1.0)))
    fall = jnp.where(degree > order_of + 1.0, fall, 0.0)
    for tile in range(padded // 8):
        rows = slice(tile * 8, tile * 8 + 8)
        left = min(8, total - tile * 8)
        entry = order_of[rows, 0:128] - start_of[rows, 0:128]
        lowest = start_of[rows, 0:128] == 0.0
        now, prev, before = [None] * z.halves, [None] * z.halves, [None] * z.halves
        for t in range(z.seg_len):
            if t > 0:
                up_by = jnp.broadcast_to(rise[rows, t : t + 1], (8, 128))
                down_by = jnp.broadcast_to(fall[rows, t : t + 1], (8, 128))
            here = entry == float(t)
            for h in range(z.halves):
                lanes = slice(h * 128, (h + 1) * 128)
                x = jnp.broadcast_to(cosine[:, lanes], (8, 128))
                if t == 0:
                    value = seed0[rows, lanes]
                elif t == 1:
                    value = jnp.where(lowest, (up_by * x) * prev[h], seed1[rows, lanes])
                else:
                    value = (up_by * x) * prev[h] - down_by * before[h]
                now[h] = jnp.where(here, first[rows, lanes], value)
                func_ref[h, pl.ds(tile * 8 * z.seg_skew + t, left, stride=z.seg_skew), :] = now[h][:left]
            before, prev, now = prev, now, [None] * z.halves
    adjoint_into(z, func_ref, ty_ref, cols, out_ref)


def make_functions(z, own, recv, ty):
    padded = up(z.seg * z.cnt, 8)
    return pl.pallas_call(
        functools.partial(functions_kernel, z),
        in_specs=[SMEM, VMEM, VMEM],
        out_specs=[VMEM] * 2,
        out_shape=[
            jax.ShapeDtypeStruct((z.halves, z.func_rows, 128), F32),
            jax.ShapeDtypeStruct(z.state, F32),
        ],
        scratch_shapes=[pltpu.VMEM((padded, z.cyc), F32)] * 3 + [pltpu.VMEM((z.state[1], 128), F32)],
        compiler_params=pltpu.CompilerParams(vmem_limit_bytes=z.limit),
        name="functions",
    )(own, recv, ty)


def total_of(z, gathered_ref):
    summed = gathered_ref[0]
    for b in range(1, z.nobs):
        summed = summed + gathered_ref[b]
    return summed, summed[2 * z.cnt : 2 * z.cnt + 1, 0:1]


def full_sum(value):
    return jnp.sum(jnp.sum(value, axis=1, keepdims=True), axis=0, keepdims=True)


def step_kernel(z, later, own_ref, *refs):
    if later:
        gathered_ref, inv_ref, func_ref, energy_ref, res_ref, dir_ref = refs[:6]
        out_ref, newres_ref, prec_ref, sol_ref, cols, pay, inv_buf, sems, inv_sems = refs[6:]
    else:
        gathered_ref, inv_ref, func_ref, sum_ref = refs[:4]
        out_ref, newres_ref, prec_ref, cols, pay, inv_buf, sems, inv_sems = refs[4:]
    fetches = [pltpu.make_async_copy(inv_ref.at[slot], inv_buf.at[slot], inv_sems.at[slot]) for slot in range(z.cnt)]
    for fetch in fetches:
        fetch.start()
    summed, curvature = total_of(z, gathered_ref)
    if later:
        step_size = energy_ref[0:1, 0:1] / curvature
        sol_ref[...] = step_size * dir_ref[...]
        newres_ref[...] = res_ref[...] - step_size * summed
    else:
        newres_ref[...] = summed
    cols[...] = jnp.zeros_like(cols)
    height = iota((8, 128), 0)
    for slot in range(z.cnt):
        fetches[slot].wait()
        vec = [
            jnp.broadcast_to(newres_ref[k * z.cnt + slot : k * z.cnt + slot + 1, 0 : z.nb], (8, z.nb)) for k in range(2)
        ]
        acc = [[jnp.zeros((8, 128), F32)] * z.halves for k in range(2)]
        for a in range(z.steps):
            block = inv_buf[slot, 8 * a : 8 * a + 8, :]
            live = height >= own_ref[slot] - 8 * a
            f = [func_ref[h, pl.ds(z.func_row(slot, a), 8), :] for h in range(z.halves)]
            for k in range(2):
                r = k * z.cnt + slot
                col = jnp.broadcast_to(jnp.sum(block * vec[k], axis=1, keepdims=True), (8, 128))
                col = jnp.where(live, col, 0.0)
                cols[8 * a : 8 * a + 8, r : r + 1] = col[:, r : r + 1]
                for h in range(z.halves):
                    acc[k][h] = acc[k][h] + f[h] * col
        for k in range(2):
            r = k * z.cnt + slot
            for h in range(z.halves):
                pay[r : r + 1, h * 128 : (h + 1) * 128] = jnp.sum(acc[k][h], axis=0, keepdims=True)
    flip(z, cols, prec_ref)
    top = 2 * z.cnt + 1
    pay[2 * z.cnt : top, :] = jnp.broadcast_to(full_sum(newres_ref[...] * prec_ref[...]), (1, z.cyc))
    if not later:
        for h in range(z.halves):
            pay[top : top + 2 * z.share, h * 128 : (h + 1) * 128] = sum_ref[h, 0 : 2 * z.share, :]
    send_copies(z, pay, out_ref, sems)


def make_step(z, own, gathered, inv, func, state, later):
    vector = jax.ShapeDtypeStruct(z.state, F32)
    outs = [pltpu.MemorySpace.HBM((z.nord, z.pay if later else z.pay_first, z.cyc), F32)] + [vector] * (2 + later)
    args = [own, gathered, inv, func] + list(state)
    return pl.pallas_call(
        functools.partial(step_kernel, z, later),
        in_specs=[SMEM, VMEM, HBM] + [VMEM] * (len(args) - 3),
        out_specs=[HBM] + [VMEM] * (len(outs) - 1),
        out_shape=outs,
        scratch_shapes=[
            pltpu.VMEM((z.state[1], 128), F32),
            pltpu.VMEM(outs[0].shape[1:], F32),
            pltpu.VMEM(inv.shape, F32),
            pltpu.SemaphoreType.DMA((z.nord,)),
            pltpu.SemaphoreType.DMA((z.cnt,)),
        ],
        compiler_params=pltpu.CompilerParams(vmem_limit_bytes=z.limit),
        name="step",
    )(*args)


def image_kernel(z, later, own_ref, ids_ref, recv_ref, func_ref, *refs):
    if later:
        tc_ref, ts_ref, old_ref, old_energy_ref, prec_ref, old_dir_ref = refs[:6]
        out_ref, energy_ref, dir_ref, val_ref, all_rows, rows, cols = refs[6:]
    else:
        out_ref, energy_ref, tc_ref, ts_ref, val_ref, all_rows, rows, cols = refs
        top = 2 * z.cnt + 1
        for o in range(z.nord):
            at = z.off + o * z.share
            for h in range(z.halves):
                lanes = slice(h * 128, (h + 1) * 128)
                tc_ref[h, at : at + z.share, :] = recv_ref[o, top : top + z.share, lanes]
                ts_ref[h, at : at + z.share, :] = recv_ref[o, top + z.share : top + 2 * z.share, lanes]

        def mirror(q, carry):
            for h in range(z.halves):
                tc_ref[h, pl.ds(z.off - q, 1), :] = tc_ref[h, pl.ds(z.off + q, 1), :]
                ts_ref[h, pl.ds(z.off - q, 1), :] = -ts_ref[h, pl.ds(z.off + q, 1), :]
            return carry

        lax.fori_loop(1, z.no, mirror, 0)
    energy = recv_ref[0, 2 * z.cnt : 2 * z.cnt + 1, 0:128]
    for o in range(1, z.nord):
        energy = energy + recv_ref[o, 2 * z.cnt : 2 * z.cnt + 1, 0:128]
    energy_ref[...] = jnp.broadcast_to(energy, (8, 128))

    def place(o, carry):
        for i in range(z.cnt):
            order = ids_ref[o * z.cnt + i]
            for k in range(2):
                r = k * z.cnt + i
                for h in range(z.halves):
                    val_ref[k, h, pl.ds(order, 1), :] = recv_ref[o, r : r + 1, h * 128 : (h + 1) * 128]
        return carry

    lax.fori_loop(0, z.nord, place, 0)
    if later:
        ratio = energy / old_energy_ref[0:1, :]
        for k in range(2):
            for h in range(z.halves):
                val_ref[k, h] = val_ref[k, h] + ratio * old_ref[k, h]
        dir_ref[...] = prec_ref[...] + ratio[:, 0:1] * old_dir_ref[...]

    def some_orders(step, carry):
        for h in range(z.halves):
            sums = [[None] * 2 for _ in range(ORDERS_AT_ONCE)]
            for tile in range(z.no // 8):
                vc, vs = val_ref[0, h, tile * 8 : tile * 8 + 8, :], val_ref[1, h, tile * 8 : tile * 8 + 8, :]
                for u in range(ORDERS_AT_ONCE):
                    m = step * ORDERS_AT_ONCE + u
                    low, high = pl.ds(z.off + tile * 8 - m, 8), pl.ds(z.off + tile * 8 + m, 8)
                    near, far = tc_ref[h, low, :], tc_ref[h, high, :]
                    snear, sfar = ts_ref[h, low, :], ts_ref[h, high, :]
                    wc = (near + far) * vc + (sfar + snear) * vs
                    ws = (sfar - snear) * vc + (near - far) * vs
                    sums[u] = [wc, ws] if tile == 0 else [sums[u][0] + wc, sums[u][1] + ws]
            for u in range(ORDERS_AT_ONCE):
                m = step * ORDERS_AT_ONCE + u
                for k in range(2):
                    all_rows[k * z.halves + h, pl.ds(m, 1), :] = 0.5 * jnp.sum(sums[u][k], axis=0, keepdims=True)
        return carry

    lax.fori_loop(0, z.no // ORDERS_AT_ONCE, some_orders, 0)
    curvature = jnp.zeros((z.no, 128), F32)
    for k in range(2):
        for h in range(z.halves):
            curvature = curvature + all_rows[k * z.halves + h] * val_ref[k, h]
    for i in range(z.cnt):
        for k in range(2):
            r = k * z.cnt + i
            for h in range(z.halves):
                rows[h, r : r + 1, :] = all_rows[k * z.halves + h, pl.ds(own_ref[i], 1), :]
    adjoint_into(z, func_ref, rows, cols, out_ref)
    out_ref[2 * z.cnt : 2 * z.cnt + 1, :] = jnp.broadcast_to(full_sum(curvature), (1, z.state[1]))


def make_image(z, own, ids, recv, func, state=()):
    later = len(state) > 0
    vector = jax.ShapeDtypeStruct(z.state, F32)
    table = jax.ShapeDtypeStruct((z.halves, z.table, 128), F32)
    outs = [vector, jax.ShapeDtypeStruct((8, 128), F32)] + ([vector] if later else [table, table])
    outs.append(jax.ShapeDtypeStruct((2, z.halves, z.no, 128), F32))
    args = [own, ids, recv, func] + list(state)
    return pl.pallas_call(
        functools.partial(image_kernel, z, later),
        in_specs=[SMEM, SMEM] + [VMEM] * (len(args) - 2),
        out_specs=[VMEM] * len(outs),
        out_shape=outs,
        scratch_shapes=[
            pltpu.VMEM((2 * z.halves, z.no, 128), F32),
            pltpu.VMEM((z.halves, z.pay, 128), F32),
            pltpu.VMEM((z.state[1], 128), F32),
        ],
        compiler_params=pltpu.CompilerParams(vmem_limit_bytes=z.limit),
        name="image",
    )(*args)


def last_kernel(z, gathered_ref, energy_ref, res_ref, sol_ref, dir_ref, out_sol, out_res):
    summed, curvature = total_of(z, gathered_ref)
    step_size = energy_ref[0:1, 0:1] / curvature
    sol = sol_ref[...] + step_size * dir_ref[...]
    res = res_ref[...] - step_size * summed
    for slot in range(z.cnt):
        for k in range(2):
            r = k * z.cnt + slot
            out_sol[slot, k : k + 1, :] = sol[r : r + 1, 0 : z.nb]
            out_res[slot, k : k + 1, :] = res[r : r + 1, 0 : z.nb]


def make_last(z, gathered, energy, res, sol, direction):
    out = jax.ShapeDtypeStruct((z.cnt, 2, z.nb), F32)
    return pl.pallas_call(
        functools.partial(last_kernel, z),
        in_specs=[VMEM] * 5,
        out_specs=[VMEM] * 2,
        out_shape=[out, out],
        compiler_params=pltpu.CompilerParams(vmem_limit_bytes=z.limit),
        name="last",
    )(gathered, energy, res, sol, direction)


def body(longitude, cycle_of, obs_count, observed, obs_weight, legendre, precond_inv, order_of_slot):
    z = Sizes(legendre, longitude.shape[1])
    dense = lambda value: value.reshape(z.rows, 128)
    legendre = pltpu.with_memory_space_constraint(legendre, pltpu.MemorySpace.HBM)
    inv = pltpu.with_memory_space_constraint(precond_inv, pltpu.MemorySpace.HBM)
    first = (lax.axis_index("ord") * z.cnt).astype(jnp.int32).reshape(1)
    seeds = make_seeds(z, first, order_of_slot, legendre)
    recv = lax.all_to_all(seeds, "ord", 0, 0)
    base = (lax.axis_index("ord") * z.share).astype(jnp.int32).reshape(1)
    sums, ty = make_tables(
        z, base, obs_count, order_of_slot, dense(longitude), dense(cycle_of), dense(observed), dense(obs_weight)
    )
    ids = recv[:, z.id_row, : z.cnt].reshape(z.no).astype(jnp.int32)
    func, part = make_functions(z, order_of_slot, recv, ty)
    gathered = lax.all_gather(part, "obs", axis=0)
    values, res, direction = make_step(z, order_of_slot, gathered, inv, func, (sums,), False)
    recv = lax.all_to_all(values, "ord", 0, 0)
    part, energy, tc, ts, all_values = make_image(z, order_of_slot, ids, recv, func)
    gathered = lax.all_gather(part, "obs", axis=0)
    values, res, prec, sol = make_step(z, order_of_slot, gathered, inv, func, (energy, res, direction), True)
    recv = lax.all_to_all(values, "ord", 0, 0)
    part, energy, direction, all_values = make_image(
        z, order_of_slot, ids, recv, func, (tc, ts, all_values, energy, prec, direction)
    )
    gathered = lax.all_gather(part, "obs", axis=0)
    return tuple(make_last(z, gathered, energy, res, sol, direction))


def solution(mesh):
    placed = (
        P("obs", None),
        P("obs", None),
        P("obs"),
        P("obs", None),
        P("obs", None),
        P("obs", "ord", None, None),
        P("ord", None, None),
        P("ord"),
    )
    return jax.shard_map(
        body,
        mesh=mesh,
        in_specs=placed,
        out_specs=(P("ord", None, None), P("ord", None, None)),
        check_vma=False,
    )
```

```python
import functools

import jax
import jax.numpy as jnp
from jax import lax
from jax.experimental import pallas as pl
from jax.experimental.pallas import tpu as pltpu
from jax.sharding import PartitionSpec as P

ITERS = 2
SEGMENTS = 2
VMEM_LIMIT = 24 << 20
WINDOW = 32
UNROLL = 4
CHUNK = 1024
F32 = jnp.float32
BF16 = jnp.bfloat16

VMEM = pl.BlockSpec(memory_space=pltpu.VMEM)
SMEM = pl.BlockSpec(memory_space=pltpu.SMEM)
HBM = pl.BlockSpec(memory_space=pltpu.MemorySpace.HBM)


def up(value, unit):
    return -(-value // unit) * unit


def iota(shape, axis):
    return lax.broadcasted_iota(jnp.int32, shape, axis)


class Sizes:
    def __init__(self, legendre, slab):
        self.cnt, self.nb, self.cyc = legendre.shape[1:]
        self.nord = lax.axis_size("ord")
        self.nobs = lax.axis_size("obs")
        self.no = self.cnt * self.nord
        self.slab = slab
        self.rows = slab // 128
        self.halves = self.cyc // 128
        self.steps = self.nb // 8
        self.state = (up(2 * self.cnt + 1, 8), up(self.nb, 128))
        self.seg = SEGMENTS
        self.seg_len = self.nb // SEGMENTS
        self.seed_rows = 2 * self.seg - 1
        self.cos_row = self.cnt * self.seed_rows
        self.id_row = self.cos_row + 1
        self.seeds = up(self.id_row + 1, 8)
        self.pay = up(2 * self.cnt + 1, 8)
        self.off = up(self.no, 8)
        self.share = -(-(2 * self.no - 1) // self.nord)
        self.freq = self.share * self.nord
        self.table = up(self.off + self.freq, 8)
        self.sums = up(2 * (self.share + self.cnt), 16)
        self.pay_first = up(2 * self.cnt + 1 + 2 * self.share, 8)
        self.width = min(CHUNK // 128, self.rows)
        self.chunks = self.rows // self.width
        self.windows = self.cyc // WINDOW
        self.skew = self.rows + 1
        self.seg_skew = self.seg_len + 1
        self.func_rows = up(self.cnt * self.seg * self.seg_skew, 8)
        self.pairs = up(self.chunks + self.windows - 1, UNROLL)
        self.sum_lanes = up(2 * self.sums, 128)
        self.limit = VMEM_LIMIT

    def func_row(self, slot, a):
        segment, at = divmod(8 * a, self.seg_len)
        return (slot * self.seg + segment) * self.seg_skew + at


def send_copies(z, source, out_ref, sems):
    copies = [pltpu.make_async_copy(source, out_ref.at[d], sems.at[d]) for d in range(z.nord)]
    for copy in copies:
        copy.start()
    for copy in copies:
        copy.wait()


def seeds_kernel(z, first_ref, own_ref, leg_ref, out_ref, stage, keep, sems, out_sems):
    copies = []

    def fetch(i, at):
        n = len(copies)
        copies.append(pltpu.make_async_copy(leg_ref.at[0, i, pl.ds(at, 8), :], stage.at[n], sems.at[n]))

    for i in range(z.cnt):
        for s in range(1, z.seg):
            fetch(i, s * z.seg_len)
        fetch(i, pl.multiple_of((first_ref[0] + i) // 8 * 8, 8))
    fetch(0, 0)
    for copy in copies:
        copy.start()
    lane = iota((z.seeds - z.id_row, z.cyc), 1)
    ids = jnp.zeros(lane.shape, F32)
    for slot in range(z.cnt):
        ids = jnp.where(lane == slot, own_ref[slot].astype(F32), ids)
    keep[z.id_row :, :] = ids
    for copy in copies:
        copy.wait()
    for i in range(z.cnt):
        base = i * z.seed_rows
        for s in range(z.seg - 1):
            keep[base + 2 * s : base + 2 * s + 2, :] = stage[i * z.seg + s, 0:2, :]
        order = first_ref[0] + i
        block = stage[i * z.seg + z.seg - 1]
        mine = iota((8, z.cyc), 0) == order - order // 8 * 8
        top = base + z.seed_rows - 1
        keep[top : top + 1, :] = jnp.sum(jnp.where(mine, block, 0.0), axis=0, keepdims=True)
    keep[z.cos_row : z.cos_row + 1, :] = stage[z.cnt * z.seg, 1:2, :]
    send_copies(z, keep, out_ref, out_sems)


def make_seeds(z, first, own, legendre):
    slabs = z.cnt * z.seg + 1
    return pl.pallas_call(
        functools.partial(seeds_kernel, z),
        in_specs=[SMEM, SMEM, HBM],
        out_specs=HBM,
        out_shape=pltpu.MemorySpace.HBM((z.nord, z.seeds, z.cyc), F32),
        scratch_shapes=[
            pltpu.VMEM((slabs, 8, z.cyc), F32),
            pltpu.VMEM((z.seeds, z.cyc), F32),
            pltpu.SemaphoreType.DMA((slabs,)),
            pltpu.SemaphoreType.DMA((z.nord,)),
        ],
        compiler_params=pltpu.CompilerParams(vmem_limit_bytes=z.limit),
        name="seeds",
    )(first, own, legendre)


def sincos(angle):
    turn = jnp.round(angle * 0.6366197723675814)
    rest = angle - turn * 1.5703125
    rest = rest - turn * 4.837512969970703e-4
    rest = rest - turn * 7.549789948768648e-8
    sq = rest * rest
    sine = rest + rest * sq * (-0.16666654611 + sq * (8.3321608736e-3 + sq * -1.9515295891e-4))
    cosine = 1.0 - 0.5 * sq + sq * sq * (4.166664568298827e-2 + sq * (-1.388731625493765e-3 + sq * 2.443315711809948e-5))
    quarter = turn.astype(jnp.int32)
    odd = (quarter & 1) == 1
    c = jnp.where(odd, sine, cosine)
    s = jnp.where(odd, cosine, sine)
    c = jnp.where(((quarter + 1) & 2) == 2, -c, c)
    s = jnp.where((quarter & 2) == 2, -s, s)
    return c, s


def split(value):
    high = value.astype(BF16)
    return high, (value - high.astype(F32)).astype(BF16)


def tables_kernel(z, base_ref, count_ref, own_ref, lon_ref, cyc_ref, data_ref, weight_ref,
                  sum_ref, ty_ref, val, powers, eights, cyc_row, lhs, hot, acc, ids, pair_chunk, pair_window, sems):
    width = z.width
    scalars = [
        pltpu.make_async_copy(cyc_ref.at[pl.ds(c * width, 1), :], ids.at[pl.ds(c, 1), :], sems.at[c])
        for c in range(z.chunks)
    ]
    for copy in scalars:
        copy.start()
    total = z.slab * z.nobs
    size = min(32, z.rows)

    def block(i, carry):
        at = pl.multiple_of(i * size, 8)
        lon = lon_ref[pl.ds(at, size), :]
        place = at * 128 + iota((size, 128), 0) * 128 + iota((size, 128), 1)
        scale = weight_ref[pl.ds(at, size), :] * (place < count_ref[0]).astype(F32) / total
        c1, s1 = sincos(lon)
        c, s = sincos(base_ref[0].astype(F32) * lon)
        c, s = c * scale, s * scale
        for p in range(z.share):
            val[pl.ds(p * z.skew + at, size), :] = c
            val[pl.ds((z.share + p) * z.skew + at, size), :] = s
            c, s = c * c1 - s * s1, s * c1 + c * s1
        scaled = scale * data_ref[pl.ds(at, size), :]
        ones, none = jnp.ones((size, 128), F32), jnp.zeros((size, 128), F32)
        c, s = ones, none
        for p in range(8):
            powers[0, p * size : p * size + size, :] = scaled * c
            powers[1, p * size : p * size + size, :] = scaled * s
            c, s = (c1, s1) if p == 0 else (c * c1 - s * s1, s * c1 + c * s1)
        c8, s8 = c, s
        c, s = ones, none
        for p in range(z.no // 8):
            eights[0, p * size : p * size + size, :] = c
            eights[1, p * size : p * size + size, :] = s
            c, s = (c8, s8) if p == 0 else (c * c8 - s * s8, s * c8 + c * s8)
        for slot in range(z.cnt):
            tens = own_ref[slot] // 8
            small = pl.ds(pl.multiple_of((own_ref[slot] - tens * 8) * size, 8), size)
            large = pl.ds(pl.multiple_of(tens * size, 8), size)
            ca, sa, cb, sb = powers[0, small, :], powers[1, small, :], eights[0, large, :], eights[1, large, :]
            val[pl.ds((2 * z.share + slot) * z.skew + at, size), :] = ca * cb - sa * sb
            val[pl.ds((2 * z.share + z.cnt + slot) * z.skew + at, size), :] = sa * cb + ca * sb
        for row in range(2 * (z.share + z.cnt), z.sums):
            val[pl.ds(row * z.skew + at, size), :] = jnp.zeros((size, 128), F32)
        cyc_row[pl.ds(at, size), :] = cyc_ref[pl.ds(at, size), :].astype(F32)
        return carry

    lax.fori_loop(0, z.rows // size, block, 0)
    acc[...] = jnp.zeros_like(acc)

    def fill(c, carry):
        for k in range(width):
            r = c * width + k
            lanes = slice(k * 128, (k + 1) * 128)
            for pair in range(z.sums // 16):
                first = val[pl.ds(pair * 16 * z.skew + r, 8, stride=z.skew), :]
                second = val[pl.ds((pair * 16 + 8) * z.skew + r, 8, stride=z.skew), :]
                high, low = split(jnp.concatenate([first, second], 0))
                lhs[c, pair * 16 : pair * 16 + 16, lanes] = high
                lhs[c, z.sums + pair * 16 : z.sums + pair * 16 + 16, lanes] = low
        return carry

    lax.fori_loop(0, z.chunks, fill, 0)
    for copy in scalars:
        copy.wait()
    for n in range(z.pairs):
        pair_chunk[n] = 0
        pair_window[n] = z.windows

    def list_chunk(c, count):
        low = ids[c, 0] // WINDOW
        following = ids[jnp.minimum(c + 1, z.chunks - 1), 0] // WINDOW
        high = jnp.where(c + 1 < z.chunks, following, z.windows - 1)

        def add(w, at):
            pair_chunk[at] = c
            pair_window[at] = w
            return at + 1

        return lax.fori_loop(low, high + 1, add, count)

    lax.fori_loop(0, z.chunks, list_chunk, 0)
    cycle_id = iota((WINDOW, 128), 0).astype(F32)

    def some(step, carry):
        for u in range(UNROLL):
            c = pair_chunk[step * UNROLL + u]
            w = pair_window[step * UNROLL + u]
            base = (w * WINDOW).astype(F32)
            for k in range(width):
                here = cyc_row[pl.ds(c * width + k, 1), :] - base
                hot[u, :, k * 128 : (k + 1) * 128] = jnp.where(cycle_id == here, 1.0, 0.0).astype(BF16)
            acc[w] += lax.dot_general(hot[u], lhs[c], (((1,), (1,)), ((), ())), preferred_element_type=F32)
        return carry

    lax.fori_loop(0, z.pairs // UNROLL, some, 0)
    both = 2 * z.share
    per_half = 128 // WINDOW
    for h in range(z.halves):
        flat = jnp.concatenate([acc[h * per_half + w] for w in range(per_half)], 0)
        flat = jnp.concatenate([flat[:, c * 128 : (c + 1) * 128].T for c in range(z.sum_lanes // 128)], 0)
        sum_ref[h, 0:both, :] = flat[0:both] + flat[z.sums : z.sums + both]
        ty_ref[h, 0 : 2 * z.cnt, :] = (
            flat[both : both + 2 * z.cnt] + flat[z.sums + both : z.sums + both + 2 * z.cnt]
        )


def make_tables(z, base, count, own, lon, cyc, data, weight):
    return pl.pallas_call(
        functools.partial(tables_kernel, z),
        in_specs=[SMEM, SMEM, SMEM] + [VMEM] * 4,
        out_specs=[VMEM] * 2,
        out_shape=[
            jax.ShapeDtypeStruct((z.halves, up(2 * z.share, 8), 128), F32),
            jax.ShapeDtypeStruct((z.halves, z.pay, 128), F32),
        ],
        scratch_shapes=[
            pltpu.VMEM((up(z.sums * z.skew, 8), 128), F32),
            pltpu.VMEM((2, 8 * min(32, z.rows), 128), F32),
            pltpu.VMEM((2, z.no // 8 * min(32, z.rows), 128), F32),
            pltpu.VMEM((z.rows, 128), F32),
            pltpu.VMEM((z.chunks, z.sum_lanes, z.width * 128), BF16),
            pltpu.VMEM((UNROLL, WINDOW, z.width * 128), BF16),
            pltpu.VMEM((z.windows + 1, WINDOW, z.sum_lanes), F32),
            pltpu.SMEM((z.chunks, 128), jnp.int32),
            pltpu.SMEM((z.pairs,), jnp.int32),
            pltpu.SMEM((z.pairs,), jnp.int32),
            pltpu.SemaphoreType.DMA((z.chunks,)),
        ],
        compiler_params=pltpu.CompilerParams(vmem_limit_bytes=2 * z.limit),
        name="tables",
    )(base, count, own, lon, cyc, data, weight)


def flip(z, cols_ref, out_ref):
    for c in range(z.state[1] // 128):
        out_ref[:, c * 128 : (c + 1) * 128] = cols_ref[c * 128 : (c + 1) * 128, :].T[0 : z.state[0]]


def adjoint_into(z, func_ref, rows_ref, cols_ref, out_ref):
    cols_ref[...] = jnp.zeros_like(cols_ref)
    for slot in range(z.cnt):
        w = [
            [
                jnp.broadcast_to(rows_ref[h, k * z.cnt + slot : k * z.cnt + slot + 1, :], (8, 128))
                for h in range(z.halves)
            ]
            for k in range(2)
        ]
        for a in range(z.steps):
            f = [func_ref[h, pl.ds(z.func_row(slot, a), 8), :] for h in range(z.halves)]
            for k in range(2):
                prod = f[0] * w[k][0]
                for h in range(1, z.halves):
                    prod = prod + f[h] * w[k][h]
                r = k * z.cnt + slot
                cols_ref[8 * a : 8 * a + 8, r : r + 1] = jnp.sum(prod, axis=1, keepdims=True)
    flip(z, cols_ref, out_ref)


def functions_kernel(z, own_ref, recv_ref, ty_ref, func_ref, out_ref, seed0, seed1, first, cols):
    total = z.seg * z.cnt
    padded = up(total, 8)
    for slot in range(z.cnt):
        order = own_ref[slot]
        block = order // z.cnt
        base = (order - block * z.cnt) * z.seed_rows
        for s in range(z.seg):
            r = slot * z.seg + s
            if s > 0:
                seed0[r : r + 1, :] = recv_ref[block, pl.ds(base + 2 * s - 2, 1), :]
                seed1[r : r + 1, :] = recv_ref[block, pl.ds(base + 2 * s - 1, 1), :]
            else:
                seed0[r : r + 1, :] = jnp.zeros((1, z.cyc), F32)
                seed1[r : r + 1, :] = jnp.zeros((1, z.cyc), F32)
            first[r : r + 1, :] = recv_ref[block, pl.ds(base + z.seed_rows - 1, 1), :]
    ground = recv_ref[0, z.seed_rows - 1 : z.seed_rows, :]
    cosine = recv_ref[0, z.cos_row : z.cos_row + 1, :] / (ground * 1.7320508075688772)
    lanes_len = up(z.seg_len, 128)
    row = iota((padded, lanes_len), 0)
    order_of = jnp.zeros(row.shape, F32)
    start_of = jnp.zeros(row.shape, F32)
    for slot in range(z.cnt):
        for s in range(z.seg):
            hit = row == slot * z.seg + s
            order_of = jnp.where(hit, own_ref[slot].astype(F32), order_of)
            start_of = jnp.where(hit, float(s * z.seg_len), start_of)
    degree = start_of + iota(row.shape, 1).astype(F32)
    minus = jnp.maximum(degree - order_of, 1.0)
    plus = jnp.maximum(degree + order_of, 1.0)
    rise = jnp.sqrt(jnp.maximum((2.0 * degree - 1.0) * (2.0 * degree + 1.0), 0.0) / (minus * plus))
    rise = jnp.where(degree > order_of, rise, 0.0)
    top = jnp.maximum((2.0 * degree + 1.0) * (degree + order_of - 1.0) * (degree - order_of - 1.0), 0.0)
    fall = jnp.sqrt(top / (minus * plus * jnp.maximum(2.0 * degree - 3.0, 1.0)))
    fall = jnp.where(degree > order_of + 1.0, fall, 0.0)
    for tile in range(padded // 8):
        rows = slice(tile * 8, tile * 8 + 8)
        left = min(8, total - tile * 8)
        entry = order_of[rows, 0:128] - start_of[rows, 0:128]
        lowest = start_of[rows, 0:128] == 0.0
        now, prev, before = [None] * z.halves, [None] * z.halves, [None] * z.halves
        for t in range(z.seg_len):
            if t > 0:
                up_by = jnp.broadcast_to(rise[rows, t : t + 1], (8, 128))
                down_by = jnp.broadcast_to(fall[rows, t : t + 1], (8, 128))
            here = entry == float(t)
            for h in range(z.halves):
                lanes = slice(h * 128, (h + 1) * 128)
                x = jnp.broadcast_to(cosine[:, lanes], (8, 128))
                if t == 0:
                    value = seed0[rows, lanes]
                elif t == 1:
                    value = jnp.where(lowest, (up_by * x) * prev[h], seed1[rows, lanes])
                else:
                    value = (up_by * x) * prev[h] - down_by * before[h]
                now[h] = jnp.where(here, first[rows, lanes], value)
                func_ref[h, pl.ds(tile * 8 * z.seg_skew + t, left, stride=z.seg_skew), :] = now[h][:left]
            before, prev, now = prev, now, [None] * z.halves
    adjoint_into(z, func_ref, ty_ref, cols, out_ref)


def make_functions(z, own, recv, ty):
    padded = up(z.seg * z.cnt, 8)
    return pl.pallas_call(
        functools.partial(functions_kernel, z),
        in_specs=[SMEM, VMEM, VMEM],
        out_specs=[VMEM] * 2,
        out_shape=[
            jax.ShapeDtypeStruct((z.halves, z.func_rows, 128), F32),
            jax.ShapeDtypeStruct(z.state, F32),
        ],
        scratch_shapes=[pltpu.VMEM((padded, z.cyc), F32)] * 3 + [pltpu.VMEM((z.state[1], 128), F32)],
        compiler_params=pltpu.CompilerParams(vmem_limit_bytes=z.limit),
        name="functions",
    )(own, recv, ty)


def total_of(z, gathered_ref):
    summed = gathered_ref[0]
    for b in range(1, z.nobs):
        summed = summed + gathered_ref[b]
    return summed, summed[2 * z.cnt : 2 * z.cnt + 1, 0:1]


def full_sum(value):
    return jnp.sum(jnp.sum(value, axis=1, keepdims=True), axis=0, keepdims=True)


def step_kernel(z, later, own_ref, *refs):
    if later:
        gathered_ref, inv_ref, func_ref, energy_ref, res_ref, dir_ref = refs[:6]
        out_ref, newres_ref, prec_ref, sol_ref, cols, pay, inv_buf, sems, inv_sems = refs[6:]
    else:
        gathered_ref, inv_ref, func_ref, sum_ref = refs[:4]
        out_ref, newres_ref, prec_ref, cols, pay, inv_buf, sems, inv_sems = refs[4:]
    fetches = [pltpu.make_async_copy(inv_ref.at[slot], inv_buf.at[slot], inv_sems.at[slot]) for slot in range(z.cnt)]
    for fetch in fetches:
        fetch.start()
    summed, curvature = total_of(z, gathered_ref)
    if later:
        step_size = energy_ref[0:1, 0:1] / curvature
        sol_ref[...] = step_size * dir_ref[...]
        newres_ref[...] = res_ref[...] - step_size * summed
    else:
        newres_ref[...] = summed
    cols[...] = jnp.zeros_like(cols)
    height = iota((8, 128), 0)
    for slot in range(z.cnt):
        fetches[slot].wait()
        vec = [
            jnp.broadcast_to(newres_ref[k * z.cnt + slot : k * z.cnt + slot + 1, 0 : z.nb], (8, z.nb)) for k in range(2)
        ]
        acc = [[jnp.zeros((8, 128), F32)] * z.halves for k in range(2)]
        for a in range(z.steps):
            block = inv_buf[slot, 8 * a : 8 * a + 8, :]
            live = height >= own_ref[slot] - 8 * a
            f = [func_ref[h, pl.ds(z.func_row(slot, a), 8), :] for h in range(z.halves)]
            for k in range(2):
                r = k * z.cnt + slot
                col = jnp.broadcast_to(jnp.sum(block * vec[k], axis=1, keepdims=True), (8, 128))
                col = jnp.where(live, col, 0.0)
                cols[8 * a : 8 * a + 8, r : r + 1] = col[:, r : r + 1]
                for h in range(z.halves):
                    acc[k][h] = acc[k][h] + f[h] * col
        for k in range(2):
            r = k * z.cnt + slot
            for h in range(z.halves):
                pay[r : r + 1, h * 128 : (h + 1) * 128] = jnp.sum(acc[k][h], axis=0, keepdims=True)
    flip(z, cols, prec_ref)
    top = 2 * z.cnt + 1
    pay[2 * z.cnt : top, :] = jnp.broadcast_to(full_sum(newres_ref[...] * prec_ref[...]), (1, z.cyc))
    if not later:
        for h in range(z.halves):
            pay[top : top + 2 * z.share, h * 128 : (h + 1) * 128] = sum_ref[h, 0 : 2 * z.share, :]
    send_copies(z, pay, out_ref, sems)


def make_step(z, own, gathered, inv, func, state, later):
    vector = jax.ShapeDtypeStruct(z.state, F32)
    outs = [pltpu.MemorySpace.HBM((z.nord, z.pay if later else z.pay_first, z.cyc), F32)] + [vector] * (2 + later)
    args = [own, gathered, inv, func] + list(state)
    return pl.pallas_call(
        functools.partial(step_kernel, z, later),
        in_specs=[SMEM, VMEM, HBM] + [VMEM] * (len(args) - 3),
        out_specs=[HBM] + [VMEM] * (len(outs) - 1),
        out_shape=outs,
        scratch_shapes=[
            pltpu.VMEM((z.state[1], 128), F32),
            pltpu.VMEM(outs[0].shape[1:], F32),
            pltpu.VMEM(inv.shape, F32),
            pltpu.SemaphoreType.DMA((z.nord,)),
            pltpu.SemaphoreType.DMA((z.cnt,)),
        ],
        compiler_params=pltpu.CompilerParams(vmem_limit_bytes=z.limit),
        name="step",
    )(*args)


def image_kernel(z, later, own_ref, ids_ref, recv_ref, func_ref, *refs):
    if later:
        tc_ref, ts_ref, old_ref, old_energy_ref, prec_ref, old_dir_ref = refs[:6]
        out_ref, energy_ref, dir_ref, val_ref, rows, cols = refs[6:]
    else:
        out_ref, energy_ref, tc_ref, ts_ref, val_ref, rows, cols = refs
        top = 2 * z.cnt + 1
        for o in range(z.nord):
            at = z.off + o * z.share
            for h in range(z.halves):
                lanes = slice(h * 128, (h + 1) * 128)
                tc_ref[h, at : at + z.share, :] = recv_ref[o, top : top + z.share, lanes]
                ts_ref[h, at : at + z.share, :] = recv_ref[o, top + z.share : top + 2 * z.share, lanes]

        def mirror(q, carry):
            for h in range(z.halves):
                tc_ref[h, pl.ds(z.off - q, 1), :] = tc_ref[h, pl.ds(z.off + q, 1), :]
                ts_ref[h, pl.ds(z.off - q, 1), :] = -ts_ref[h, pl.ds(z.off + q, 1), :]
            return carry

        lax.fori_loop(1, z.no, mirror, 0)
    energy = recv_ref[0, 2 * z.cnt : 2 * z.cnt + 1, 0:128]
    for o in range(1, z.nord):
        energy = energy + recv_ref[o, 2 * z.cnt : 2 * z.cnt + 1, 0:128]
    energy_ref[...] = jnp.broadcast_to(energy, (8, 128))

    def place(o, carry):
        for i in range(z.cnt):
            order = ids_ref[o * z.cnt + i]
            for k in range(2):
                r = k * z.cnt + i
                for h in range(z.halves):
                    val_ref[k, h, pl.ds(order, 1), :] = recv_ref[o, r : r + 1, h * 128 : (h + 1) * 128]
        return carry

    lax.fori_loop(0, z.nord, place, 0)
    if later:
        ratio = energy / old_energy_ref[0:1, :]
        for k in range(2):
            for h in range(z.halves):
                val_ref[k, h] = val_ref[k, h] + ratio * old_ref[k, h]
        dir_ref[...] = prec_ref[...] + ratio[:, 0:1] * old_dir_ref[...]

    tiles = z.no // 8

    def sums_of(m, h, chosen):
        both = None
        for tile in chosen:
            vc, vs = val_ref[0, h, tile * 8 : tile * 8 + 8, :], val_ref[1, h, tile * 8 : tile * 8 + 8, :]
            low, high = pl.ds(z.off + tile * 8 - m, 8), pl.ds(z.off + tile * 8 + m, 8)
            near, far = tc_ref[h, low, :], tc_ref[h, high, :]
            snear, sfar = ts_ref[h, low, :], ts_ref[h, high, :]
            wc = (near + far) * vc + (sfar + snear) * vs
            ws = (sfar - snear) * vc + (near - far) * vs
            both = (wc, ws) if both is None else (both[0] + wc, both[1] + ws)
        return both

    for i in range(z.cnt):
        for h in range(z.halves):
            for k, value in enumerate(sums_of(own_ref[i], h, range(tiles))):
                r = k * z.cnt + i
                rows[h, r : r + 1, :] = 0.5 * jnp.sum(value, axis=0, keepdims=True)

    def times_row(m, h, value):
        at = pl.ds(m, 1)
        return val_ref[0, h, at, :] * value[0] + val_ref[1, h, at, :] * value[1]

    curvature = jnp.zeros((8, 128), F32)
    if z.no <= 128:
        for m in range(z.no):
            for h in range(z.halves):
                value = sums_of(m, h, [m // 8])
                if m // 8 + 1 < tiles:
                    above = sums_of(m, h, range(m // 8 + 1, tiles))
                    value = [v + 2.0 * w for v, w in zip(value, above)]
                curvature = curvature + times_row(m, h, value)
    else:

        def one_order(m, total):
            for h in range(z.halves):
                total = total + times_row(m, h, sums_of(m, h, range(tiles)))
            return total

        curvature = lax.fori_loop(0, z.no, one_order, curvature)
    curvature = 0.5 * curvature
    adjoint_into(z, func_ref, rows, cols, out_ref)
    out_ref[2 * z.cnt : 2 * z.cnt + 1, :] = jnp.broadcast_to(full_sum(curvature), (1, z.state[1]))


def make_image(z, own, ids, recv, func, state=()):
    later = len(state) > 0
    vector = jax.ShapeDtypeStruct(z.state, F32)
    table = jax.ShapeDtypeStruct((z.halves, z.table, 128), F32)
    outs = [vector, jax.ShapeDtypeStruct((8, 128), F32)] + ([vector] if later else [table, table])
    outs.append(jax.ShapeDtypeStruct((2, z.halves, z.no, 128), F32))
    args = [own, ids, recv, func] + list(state)
    return pl.pallas_call(
        functools.partial(image_kernel, z, later),
        in_specs=[SMEM, SMEM] + [VMEM] * (len(args) - 2),
        out_specs=[VMEM] * len(outs),
        out_shape=outs,
        scratch_shapes=[
            pltpu.VMEM((z.halves, z.pay, 128), F32),
            pltpu.VMEM((z.state[1], 128), F32),
        ],
        compiler_params=pltpu.CompilerParams(vmem_limit_bytes=z.limit),
        name="image",
    )(*args)


def last_kernel(z, gathered_ref, energy_ref, res_ref, sol_ref, dir_ref, out_sol, out_res):
    summed, curvature = total_of(z, gathered_ref)
    step_size = energy_ref[0:1, 0:1] / curvature
    sol = sol_ref[...] + step_size * dir_ref[...]
    res = res_ref[...] - step_size * summed
    for slot in range(z.cnt):
        for k in range(2):
            r = k * z.cnt + slot
            out_sol[slot, k : k + 1, :] = sol[r : r + 1, 0 : z.nb]
            out_res[slot, k : k + 1, :] = res[r : r + 1, 0 : z.nb]


def make_last(z, gathered, energy, res, sol, direction):
    out = jax.ShapeDtypeStruct((z.cnt, 2, z.nb), F32)
    return pl.pallas_call(
        functools.partial(last_kernel, z),
        in_specs=[VMEM] * 5,
        out_specs=[VMEM] * 2,
        out_shape=[out, out],
        compiler_params=pltpu.CompilerParams(vmem_limit_bytes=z.limit),
        name="last",
    )(gathered, energy, res, sol, direction)


def body(longitude, cycle_of, obs_count, observed, obs_weight, legendre, precond_inv, order_of_slot):
    z = Sizes(legendre, longitude.shape[1])
    dense = lambda value: value.reshape(z.rows, 128)
    legendre = pltpu.with_memory_space_constraint(legendre, pltpu.MemorySpace.HBM)
    inv = pltpu.with_memory_space_constraint(precond_inv, pltpu.MemorySpace.HBM)
    first = (lax.axis_index("ord") * z.cnt).astype(jnp.int32).reshape(1)
    seeds = make_seeds(z, first, order_of_slot, legendre)
    recv = lax.all_to_all(seeds, "ord", 0, 0)
    base = (lax.axis_index("ord") * z.share).astype(jnp.int32).reshape(1)
    sums, ty = make_tables(
        z, base, obs_count, order_of_slot, dense(longitude), dense(cycle_of), dense(observed), dense(obs_weight)
    )
    ids = recv[:, z.id_row, : z.cnt].reshape(z.no).astype(jnp.int32)
    func, part = make_functions(z, order_of_slot, recv, ty)
    gathered = lax.all_gather(part, "obs", axis=0)
    values, res, direction = make_step(z, order_of_slot, gathered, inv, func, (sums,), False)
    recv = lax.all_to_all(values, "ord", 0, 0)
    part, energy, tc, ts, all_values = make_image(z, order_of_slot, ids, recv, func)
    gathered = lax.all_gather(part, "obs", axis=0)
    values, res, prec, sol = make_step(z, order_of_slot, gathered, inv, func, (energy, res, direction), True)
    recv = lax.all_to_all(values, "ord", 0, 0)
    part, energy, direction, all_values = make_image(
        z, order_of_slot, ids, recv, func, (tc, ts, all_values, energy, prec, direction)
    )
    gathered = lax.all_gather(part, "obs", axis=0)
    return tuple(make_last(z, gathered, energy, res, sol, direction))


def solution(mesh):
    placed = (
        P("obs", None),
        P("obs", None),
        P("obs"),
        P("obs", None),
        P("obs", None),
        P("obs", "ord", None, None),
        P("ord", None, None),
        P("ord"),
    )
    return jax.shard_map(
        body,
        mesh=mesh,
        in_specs=placed,
        out_specs=(P("ord", None, None), P("ord", None, None)),
        check_vma=False,
    )
```

```python
import functools

import jax
import jax.numpy as jnp
from jax import lax
from jax.experimental import pallas as pl
from jax.experimental.pallas import tpu as pltpu
from jax.sharding import PartitionSpec as P

ITERS = 2
SEGMENTS = 2
VMEM_LIMIT = 24 << 20
WINDOW = 32
UNROLL = 8
CHUNK = 1024
F32 = jnp.float32
BF16 = jnp.bfloat16

VMEM = pl.BlockSpec(memory_space=pltpu.VMEM)
SMEM = pl.BlockSpec(memory_space=pltpu.SMEM)
HBM = pl.BlockSpec(memory_space=pltpu.MemorySpace.HBM)


def up(value, unit):
    return -(-value // unit) * unit


def iota(shape, axis):
    return lax.broadcasted_iota(jnp.int32, shape, axis)


class Sizes:
    def __init__(self, legendre, slab):
        self.cnt, self.nb, self.cyc = legendre.shape[1:]
        self.nord = lax.axis_size("ord")
        self.nobs = lax.axis_size("obs")
        self.no = self.cnt * self.nord
        self.slab = slab
        self.rows = slab // 128
        self.halves = self.cyc // 128
        self.steps = self.nb // 8
        self.state = (up(2 * self.cnt + 1, 8), up(self.nb, 128))
        self.seg = SEGMENTS
        self.seg_len = self.nb // SEGMENTS
        self.seed_rows = 2 * self.seg - 1
        self.cos_row = self.cnt * self.seed_rows
        self.id_row = self.cos_row + 1
        self.seeds = up(self.id_row + 1, 8)
        self.pay = up(2 * self.cnt + 1, 8)
        self.off = up(self.no, 8)
        self.share = -(-(2 * self.no - 1) // self.nord)
        self.freq = self.share * self.nord
        self.table = up(self.off + self.freq, 8)
        self.sums = up(2 * (self.share + self.cnt), 16)
        self.pay_first = up(2 * self.cnt + 1 + 2 * self.share, 8)
        self.width = min(CHUNK // 128, self.rows)
        self.chunks = self.rows // self.width
        self.windows = self.cyc // WINDOW
        self.skew = self.rows + 1
        self.seg_skew = self.seg_len + 1
        self.func_rows = up(self.cnt * self.seg * self.seg_skew, 8)
        self.pairs = up(self.chunks + self.windows - 1, UNROLL)
        self.sum_lanes = up(2 * self.sums, 128)
        self.limit = VMEM_LIMIT

    def func_row(self, slot, a):
        segment, at = divmod(8 * a, self.seg_len)
        return (slot * self.seg + segment) * self.seg_skew + at


def send_copies(z, source, out_ref, sems):
    copies = [pltpu.make_async_copy(source, out_ref.at[d], sems.at[d]) for d in range(z.nord)]
    for copy in copies:
        copy.start()
    for copy in copies:
        copy.wait()


def seeds_kernel(z, first_ref, own_ref, leg_ref, *refs):
    held, (out_ref, *near), (stage, keep, sems, out_sems, near_sems) = refs[:4], refs[4:9], refs[9:]
    copies = []

    def fetch(i, at):
        n = len(copies)
        copies.append(pltpu.make_async_copy(leg_ref.at[0, i, pl.ds(at, 8), :], stage.at[n], sems.at[n]))

    for i in range(z.cnt):
        for s in range(1, z.seg):
            fetch(i, s * z.seg_len)
        fetch(i, pl.multiple_of((first_ref[0] + i) // 8 * 8, 8))
    fetch(0, 0)
    for copy in copies:
        copy.start()
    moves = [pltpu.make_async_copy(held[n], near[n], near_sems.at[n]) for n in range(4)]
    for move in moves:
        move.start()
    lane = iota((z.seeds - z.id_row, z.cyc), 1)
    ids = jnp.zeros(lane.shape, F32)
    for slot in range(z.cnt):
        ids = jnp.where(lane == slot, own_ref[slot].astype(F32), ids)
    keep[z.id_row :, :] = ids
    for copy in copies:
        copy.wait()
    for i in range(z.cnt):
        base = i * z.seed_rows
        for s in range(z.seg - 1):
            keep[base + 2 * s : base + 2 * s + 2, :] = stage[i * z.seg + s, 0:2, :]
        order = first_ref[0] + i
        block = stage[i * z.seg + z.seg - 1]
        mine = iota((8, z.cyc), 0) == order - order // 8 * 8
        top = base + z.seed_rows - 1
        keep[top : top + 1, :] = jnp.sum(jnp.where(mine, block, 0.0), axis=0, keepdims=True)
    keep[z.cos_row : z.cos_row + 1, :] = stage[z.cnt * z.seg, 1:2, :]
    send_copies(z, keep, out_ref, out_sems)
    for move in moves:
        move.wait()


def make_seeds(z, first, own, legendre, held):
    slabs = z.cnt * z.seg + 1
    return pl.pallas_call(
        functools.partial(seeds_kernel, z),
        in_specs=[SMEM, SMEM, HBM] + [HBM] * 4,
        out_specs=[HBM] + [VMEM] * 4,
        out_shape=[pltpu.MemorySpace.HBM((z.nord, z.seeds, z.cyc), F32)]
        + [jax.ShapeDtypeStruct(value.shape, value.dtype) for value in held],
        scratch_shapes=[
            pltpu.VMEM((slabs, 8, z.cyc), F32),
            pltpu.VMEM((z.seeds, z.cyc), F32),
            pltpu.SemaphoreType.DMA((slabs,)),
            pltpu.SemaphoreType.DMA((z.nord,)),
            pltpu.SemaphoreType.DMA((4,)),
        ],
        compiler_params=pltpu.CompilerParams(vmem_limit_bytes=z.limit),
        name="seeds",
    )(first, own, legendre, *held)


def sincos(angle):
    turn = jnp.round(angle * 0.6366197723675814)
    rest = angle - turn * 1.5703125
    rest = rest - turn * 4.837512969970703e-4
    rest = rest - turn * 7.549789948768648e-8
    sq = rest * rest
    sine = rest + rest * sq * (-0.16666654611 + sq * (8.3321608736e-3 + sq * -1.9515295891e-4))
    cosine = 1.0 - 0.5 * sq + sq * sq * (4.166664568298827e-2 + sq * (-1.388731625493765e-3 + sq * 2.443315711809948e-5))
    quarter = turn.astype(jnp.int32)
    odd = (quarter & 1) == 1
    c = jnp.where(odd, sine, cosine)
    s = jnp.where(odd, cosine, sine)
    c = jnp.where(((quarter + 1) & 2) == 2, -c, c)
    s = jnp.where((quarter & 2) == 2, -s, s)
    return c, s


def split(value):
    high = value.astype(BF16)
    return high, (value - high.astype(F32)).astype(BF16)


def tables_kernel(z, base_ref, count_ref, own_ref, lon_ref, cyc_ref, data_ref, weight_ref,
                  sum_ref, ty_ref, val, powers, eights, cyc_row, lhs, hot, acc, ids, pair_chunk, pair_window, sems):
    width = z.width
    scalars = [
        pltpu.make_async_copy(cyc_ref.at[pl.ds(c * width, 1), :], ids.at[pl.ds(c, 1), :], sems.at[c])
        for c in range(z.chunks)
    ]
    for copy in scalars:
        copy.start()
    total = z.slab * z.nobs
    size = min(32, z.rows)

    def block(i, carry):
        at = pl.multiple_of(i * size, 8)
        lon = lon_ref[pl.ds(at, size), :]
        place = at * 128 + iota((size, 128), 0) * 128 + iota((size, 128), 1)
        scale = weight_ref[pl.ds(at, size), :] * (place < count_ref[0]).astype(F32) / total
        c1, s1 = sincos(lon)
        c, s = sincos(base_ref[0].astype(F32) * lon)
        c, s = c * scale, s * scale
        for p in range(z.share):
            val[pl.ds(p * z.skew + at, size), :] = c
            val[pl.ds((z.share + p) * z.skew + at, size), :] = s
            c, s = c * c1 - s * s1, s * c1 + c * s1
        scaled = scale * data_ref[pl.ds(at, size), :]
        ones, none = jnp.ones((size, 128), F32), jnp.zeros((size, 128), F32)
        c, s = ones, none
        for p in range(8):
            powers[0, p * size : p * size + size, :] = scaled * c
            powers[1, p * size : p * size + size, :] = scaled * s
            c, s = (c1, s1) if p == 0 else (c * c1 - s * s1, s * c1 + c * s1)
        c8, s8 = c, s
        c, s = ones, none
        for p in range(z.no // 8):
            eights[0, p * size : p * size + size, :] = c
            eights[1, p * size : p * size + size, :] = s
            c, s = (c8, s8) if p == 0 else (c * c8 - s * s8, s * c8 + c * s8)
        for slot in range(z.cnt):
            tens = own_ref[slot] // 8
            small = pl.ds(pl.multiple_of((own_ref[slot] - tens * 8) * size, 8), size)
            large = pl.ds(pl.multiple_of(tens * size, 8), size)
            ca, sa, cb, sb = powers[0, small, :], powers[1, small, :], eights[0, large, :], eights[1, large, :]
            val[pl.ds((2 * z.share + slot) * z.skew + at, size), :] = ca * cb - sa * sb
            val[pl.ds((2 * z.share + z.cnt + slot) * z.skew + at, size), :] = sa * cb + ca * sb
        for row in range(2 * (z.share + z.cnt), z.sums):
            val[pl.ds(row * z.skew + at, size), :] = jnp.zeros((size, 128), F32)
        cyc_row[pl.ds(at, size), :] = cyc_ref[pl.ds(at, size), :].astype(F32)
        return carry

    lax.fori_loop(0, z.rows // size, block, 0)
    acc[...] = jnp.zeros_like(acc)

    def fill(c, carry):
        for k in range(width):
            r = c * width + k
            lanes = slice(k * 128, (k + 1) * 128)
            for pair in range(z.sums // 16):
                first = val[pl.ds(pair * 16 * z.skew + r, 8, stride=z.skew), :]
                second = val[pl.ds((pair * 16 + 8) * z.skew + r, 8, stride=z.skew), :]
                high, low = split(jnp.concatenate([first, second], 0))
                lhs[c, pair * 16 : pair * 16 + 16, lanes] = high
                lhs[c, z.sums + pair * 16 : z.sums + pair * 16 + 16, lanes] = low
        return carry

    lax.fori_loop(0, z.chunks, fill, 0)
    for copy in scalars:
        copy.wait()
    for n in range(z.pairs):
        pair_chunk[n] = 0
        pair_window[n] = z.windows

    def list_chunk(c, count):
        low = ids[c, 0] // WINDOW
        following = ids[jnp.minimum(c + 1, z.chunks - 1), 0] // WINDOW
        high = jnp.where(c + 1 < z.chunks, following, z.windows - 1)

        def add(w, at):
            pair_chunk[at] = c
            pair_window[at] = w
            return at + 1

        return lax.fori_loop(low, high + 1, add, count)

    lax.fori_loop(0, z.chunks, list_chunk, 0)
    cycle_id = iota((WINDOW, 128), 0).astype(F32)

    def some(step, carry):
        for u in range(UNROLL):
            c = pair_chunk[step * UNROLL + u]
            w = pair_window[step * UNROLL + u]
            base = (w * WINDOW).astype(F32)
            for k in range(width):
                here = cyc_row[pl.ds(c * width + k, 1), :] - base
                hot[u, :, k * 128 : (k + 1) * 128] = jnp.where(cycle_id == here, 1.0, 0.0).astype(BF16)
            acc[w] += lax.dot_general(hot[u], lhs[c], (((1,), (1,)), ((), ())), preferred_element_type=F32)
        return carry

    lax.fori_loop(0, z.pairs // UNROLL, some, 0)
    both = 2 * z.share
    per_half = 128 // WINDOW
    for h in range(z.halves):
        flat = jnp.concatenate([acc[h * per_half + w] for w in range(per_half)], 0)
        flat = jnp.concatenate([flat[:, c * 128 : (c + 1) * 128].T for c in range(z.sum_lanes // 128)], 0)
        sum_ref[h, 0:both, :] = flat[0:both] + flat[z.sums : z.sums + both]
        ty_ref[h, 0 : 2 * z.cnt, :] = (
            flat[both : both + 2 * z.cnt] + flat[z.sums + both : z.sums + both + 2 * z.cnt]
        )


def make_tables(z, base, count, own, lon, cyc, data, weight):
    return pl.pallas_call(
        functools.partial(tables_kernel, z),
        in_specs=[SMEM, SMEM, SMEM] + [VMEM] * 4,
        out_specs=[VMEM] * 2,
        out_shape=[
            jax.ShapeDtypeStruct((z.halves, up(2 * z.share, 8), 128), F32),
            jax.ShapeDtypeStruct((z.halves, z.pay, 128), F32),
        ],
        scratch_shapes=[
            pltpu.VMEM((up(z.sums * z.skew, 8), 128), F32),
            pltpu.VMEM((2, 8 * min(32, z.rows), 128), F32),
            pltpu.VMEM((2, z.no // 8 * min(32, z.rows), 128), F32),
            pltpu.VMEM((z.rows, 128), F32),
            pltpu.VMEM((z.chunks, z.sum_lanes, z.width * 128), BF16),
            pltpu.VMEM((UNROLL, WINDOW, z.width * 128), BF16),
            pltpu.VMEM((z.windows + 1, WINDOW, z.sum_lanes), F32),
            pltpu.SMEM((z.chunks, 128), jnp.int32),
            pltpu.SMEM((z.pairs,), jnp.int32),
            pltpu.SMEM((z.pairs,), jnp.int32),
            pltpu.SemaphoreType.DMA((z.chunks,)),
        ],
        compiler_params=pltpu.CompilerParams(vmem_limit_bytes=2 * z.limit),
        name="tables",
    )(base, count, own, lon, cyc, data, weight)


def flip(z, cols_ref, out_ref):
    for c in range(z.state[1] // 128):
        out_ref[:, c * 128 : (c + 1) * 128] = cols_ref[c * 128 : (c + 1) * 128, :].T[0 : z.state[0]]


def adjoint_into(z, func_ref, rows_ref, cols_ref, out_ref):
    cols_ref[...] = jnp.zeros_like(cols_ref)
    for slot in range(z.cnt):
        w = [
            [
                jnp.broadcast_to(rows_ref[h, k * z.cnt + slot : k * z.cnt + slot + 1, :], (8, 128))
                for h in range(z.halves)
            ]
            for k in range(2)
        ]
        for a in range(z.steps):
            f = [func_ref[h, pl.ds(z.func_row(slot, a), 8), :] for h in range(z.halves)]
            for k in range(2):
                prod = f[0] * w[k][0]
                for h in range(1, z.halves):
                    prod = prod + f[h] * w[k][h]
                r = k * z.cnt + slot
                cols_ref[8 * a : 8 * a + 8, r : r + 1] = jnp.sum(prod, axis=1, keepdims=True)
    flip(z, cols_ref, out_ref)


def functions_kernel(z, own_ref, recv_ref, ty_ref, inv_ref, func_ref, out_ref, inv_out, seed0, seed1, first, cols, sem):
    fetch = pltpu.make_async_copy(inv_ref, inv_out, sem.at[0])
    fetch.start()
    total = z.seg * z.cnt
    padded = up(total, 8)
    for slot in range(z.cnt):
        order = own_ref[slot]
        block = order // z.cnt
        base = (order - block * z.cnt) * z.seed_rows
        for s in range(z.seg):
            r = slot * z.seg + s
            if s > 0:
                seed0[r : r + 1, :] = recv_ref[block, pl.ds(base + 2 * s - 2, 1), :]
                seed1[r : r + 1, :] = recv_ref[block, pl.ds(base + 2 * s - 1, 1), :]
            else:
                seed0[r : r + 1, :] = jnp.zeros((1, z.cyc), F32)
                seed1[r : r + 1, :] = jnp.zeros((1, z.cyc), F32)
            first[r : r + 1, :] = recv_ref[block, pl.ds(base + z.seed_rows - 1, 1), :]
    ground = recv_ref[0, z.seed_rows - 1 : z.seed_rows, :]
    cosine = recv_ref[0, z.cos_row : z.cos_row + 1, :] / (ground * 1.7320508075688772)
    lanes_len = up(z.seg_len, 128)
    row = iota((padded, lanes_len), 0)
    order_of = jnp.zeros(row.shape, F32)
    start_of = jnp.zeros(row.shape, F32)
    for slot in range(z.cnt):
        for s in range(z.seg):
            hit = row == slot * z.seg + s
            order_of = jnp.where(hit, own_ref[slot].astype(F32), order_of)
            start_of = jnp.where(hit, float(s * z.seg_len), start_of)
    degree = start_of + iota(row.shape, 1).astype(F32)
    minus = jnp.maximum(degree - order_of, 1.0)
    plus = jnp.maximum(degree + order_of, 1.0)
    rise = jnp.sqrt(jnp.maximum((2.0 * degree - 1.0) * (2.0 * degree + 1.0), 0.0) / (minus * plus))
    rise = jnp.where(degree > order_of, rise, 0.0)
    top = jnp.maximum((2.0 * degree + 1.0) * (degree + order_of - 1.0) * (degree - order_of - 1.0), 0.0)
    fall = jnp.sqrt(top / (minus * plus * jnp.maximum(2.0 * degree - 3.0, 1.0)))
    fall = jnp.where(degree > order_of + 1.0, fall, 0.0)
    for tile in range(padded // 8):
        rows = slice(tile * 8, tile * 8 + 8)
        left = min(8, total - tile * 8)
        entry = order_of[rows, 0:128] - start_of[rows, 0:128]
        lowest = start_of[rows, 0:128] == 0.0
        now, prev, before = [None] * z.halves, [None] * z.halves, [None] * z.halves
        for t in range(z.seg_len):
            if t > 0:
                up_by = jnp.broadcast_to(rise[rows, t : t + 1], (8, 128))
                down_by = jnp.broadcast_to(fall[rows, t : t + 1], (8, 128))
            here = entry == float(t)
            for h in range(z.halves):
                lanes = slice(h * 128, (h + 1) * 128)
                x = jnp.broadcast_to(cosine[:, lanes], (8, 128))
                if t == 0:
                    value = seed0[rows, lanes]
                elif t == 1:
                    value = jnp.where(lowest, (up_by * x) * prev[h], seed1[rows, lanes])
                else:
                    value = (up_by * x) * prev[h] - down_by * before[h]
                now[h] = jnp.where(here, first[rows, lanes], value)
                func_ref[h, pl.ds(tile * 8 * z.seg_skew + t, left, stride=z.seg_skew), :] = now[h][:left]
            before, prev, now = prev, now, [None] * z.halves
    adjoint_into(z, func_ref, ty_ref, cols, out_ref)
    fetch.wait()


def make_functions(z, own, recv, ty, inv):
    padded = up(z.seg * z.cnt, 8)
    return pl.pallas_call(
        functools.partial(functions_kernel, z),
        in_specs=[SMEM, VMEM, VMEM, HBM],
        out_specs=[VMEM] * 3,
        out_shape=[
            jax.ShapeDtypeStruct((z.halves, z.func_rows, 128), F32),
            jax.ShapeDtypeStruct(z.state, F32),
            jax.ShapeDtypeStruct(inv.shape, F32),
        ],
        scratch_shapes=[pltpu.VMEM((padded, z.cyc), F32)] * 3
        + [pltpu.VMEM((z.state[1], 128), F32), pltpu.SemaphoreType.DMA((1,))],
        compiler_params=pltpu.CompilerParams(vmem_limit_bytes=z.limit),
        name="functions",
    )(own, recv, ty, inv)


def total_of(z, gathered_ref):
    summed = gathered_ref[0]
    for b in range(1, z.nobs):
        summed = summed + gathered_ref[b]
    return summed, summed[2 * z.cnt : 2 * z.cnt + 1, 0:1]


def full_sum(value):
    return jnp.sum(jnp.sum(value, axis=1, keepdims=True), axis=0, keepdims=True)


def step_kernel(z, later, own_ref, *refs):
    if later:
        gathered_ref, inv_ref, func_ref, energy_ref, res_ref, dir_ref = refs[:6]
        out_ref, newres_ref, prec_ref, sol_ref, cols, pay, sems = refs[6:]
    else:
        gathered_ref, inv_ref, func_ref, sum_ref = refs[:4]
        out_ref, newres_ref, prec_ref, cols, pay, sems = refs[4:]
    summed, curvature = total_of(z, gathered_ref)
    if later:
        step_size = energy_ref[0:1, 0:1] / curvature
        sol_ref[...] = step_size * dir_ref[...]
        newres_ref[...] = res_ref[...] - step_size * summed
    else:
        newres_ref[...] = summed
    cols[...] = jnp.zeros_like(cols)
    height = iota((8, 128), 0)
    for slot in range(z.cnt):
        vec = [
            jnp.broadcast_to(newres_ref[k * z.cnt + slot : k * z.cnt + slot + 1, 0 : z.nb], (8, z.nb)) for k in range(2)
        ]
        acc = [[jnp.zeros((8, 128), F32)] * z.halves for k in range(2)]
        for a in range(z.steps):
            block = inv_ref[slot, 8 * a : 8 * a + 8, :]
            live = height >= own_ref[slot] - 8 * a
            f = [func_ref[h, pl.ds(z.func_row(slot, a), 8), :] for h in range(z.halves)]
            for k in range(2):
                r = k * z.cnt + slot
                col = jnp.broadcast_to(jnp.sum(block * vec[k], axis=1, keepdims=True), (8, 128))
                col = jnp.where(live, col, 0.0)
                cols[8 * a : 8 * a + 8, r : r + 1] = col[:, r : r + 1]
                for h in range(z.halves):
                    acc[k][h] = acc[k][h] + f[h] * col
        for k in range(2):
            r = k * z.cnt + slot
            for h in range(z.halves):
                pay[r : r + 1, h * 128 : (h + 1) * 128] = jnp.sum(acc[k][h], axis=0, keepdims=True)
    flip(z, cols, prec_ref)
    top = 2 * z.cnt + 1
    pay[2 * z.cnt : top, :] = jnp.broadcast_to(full_sum(newres_ref[...] * prec_ref[...]), (1, z.cyc))
    if not later:
        for h in range(z.halves):
            pay[top : top + 2 * z.share, h * 128 : (h + 1) * 128] = sum_ref[h, 0 : 2 * z.share, :]
    send_copies(z, pay, out_ref, sems)


def make_step(z, own, gathered, inv, func, state, later):
    vector = jax.ShapeDtypeStruct(z.state, F32)
    outs = [pltpu.MemorySpace.HBM((z.nord, z.pay if later else z.pay_first, z.cyc), F32)] + [vector] * (2 + later)
    args = [own, gathered, inv, func] + list(state)
    return pl.pallas_call(
        functools.partial(step_kernel, z, later),
        in_specs=[SMEM] + [VMEM] * (len(args) - 1),
        out_specs=[HBM] + [VMEM] * (len(outs) - 1),
        out_shape=outs,
        scratch_shapes=[
            pltpu.VMEM((z.state[1], 128), F32),
            pltpu.VMEM(outs[0].shape[1:], F32),
            pltpu.SemaphoreType.DMA((z.nord,)),
        ],
        compiler_params=pltpu.CompilerParams(vmem_limit_bytes=z.limit),
        name="step",
    )(*args)


def image_kernel(z, later, own_ref, ids_ref, recv_ref, func_ref, *refs):
    if later:
        tc_ref, ts_ref, old_ref, old_energy_ref, prec_ref, old_dir_ref = refs[:6]
        out_ref, energy_ref, dir_ref, val_ref, rows, cols = refs[6:]
    else:
        inv_ref, out_ref, energy_ref, tc_ref, ts_ref, val_ref, inv_out, rows, cols, sem = refs
        fetch = pltpu.make_async_copy(inv_ref, inv_out, sem.at[0])
        fetch.start()
        top = 2 * z.cnt + 1
        for o in range(z.nord):
            at = z.off + o * z.share
            for h in range(z.halves):
                lanes = slice(h * 128, (h + 1) * 128)
                tc_ref[h, at : at + z.share, :] = recv_ref[o, top : top + z.share, lanes]
                ts_ref[h, at : at + z.share, :] = recv_ref[o, top + z.share : top + 2 * z.share, lanes]

        def mirror(q, carry):
            for h in range(z.halves):
                tc_ref[h, pl.ds(z.off - q, 1), :] = tc_ref[h, pl.ds(z.off + q, 1), :]
                ts_ref[h, pl.ds(z.off - q, 1), :] = -ts_ref[h, pl.ds(z.off + q, 1), :]
            return carry

        lax.fori_loop(1, z.no, mirror, 0)
    energy = recv_ref[0, 2 * z.cnt : 2 * z.cnt + 1, 0:128]
    for o in range(1, z.nord):
        energy = energy + recv_ref[o, 2 * z.cnt : 2 * z.cnt + 1, 0:128]
    energy_ref[...] = jnp.broadcast_to(energy, (8, 128))

    def place(o, carry):
        for i in range(z.cnt):
            order = ids_ref[o * z.cnt + i]
            for k in range(2):
                r = k * z.cnt + i
                for h in range(z.halves):
                    val_ref[k, h, pl.ds(order, 1), :] = recv_ref[o, r : r + 1, h * 128 : (h + 1) * 128]
        return carry

    lax.fori_loop(0, z.nord, place, 0)
    if later:
        ratio = energy / old_energy_ref[0:1, :]
        for k in range(2):
            for h in range(z.halves):
                val_ref[k, h] = val_ref[k, h] + ratio * old_ref[k, h]
        dir_ref[...] = prec_ref[...] + ratio[:, 0:1] * old_dir_ref[...]

    tiles = z.no // 8

    def sums_of(m, h, chosen):
        both = None
        for tile in chosen:
            vc, vs = val_ref[0, h, tile * 8 : tile * 8 + 8, :], val_ref[1, h, tile * 8 : tile * 8 + 8, :]
            low, high = pl.ds(z.off + tile * 8 - m, 8), pl.ds(z.off + tile * 8 + m, 8)
            near, far = tc_ref[h, low, :], tc_ref[h, high, :]
            snear, sfar = ts_ref[h, low, :], ts_ref[h, high, :]
            wc = (near + far) * vc + (sfar + snear) * vs
            ws = (sfar - snear) * vc + (near - far) * vs
            both = (wc, ws) if both is None else (both[0] + wc, both[1] + ws)
        return both

    for i in range(z.cnt):
        for h in range(z.halves):
            for k, value in enumerate(sums_of(own_ref[i], h, range(tiles))):
                r = k * z.cnt + i
                rows[h, r : r + 1, :] = 0.5 * jnp.sum(value, axis=0, keepdims=True)

    def times_row(m, h, value):
        at = pl.ds(m, 1)
        return val_ref[0, h, at, :] * value[0] + val_ref[1, h, at, :] * value[1]

    curvature = jnp.zeros((8, 128), F32)
    if z.no <= 128:
        for m in range(z.no):
            for h in range(z.halves):
                value = sums_of(m, h, [m // 8])
                if m // 8 + 1 < tiles:
                    above = sums_of(m, h, range(m // 8 + 1, tiles))
                    value = [v + 2.0 * w for v, w in zip(value, above)]
                curvature = curvature + times_row(m, h, value)
    else:

        def one_order(m, total):
            for h in range(z.halves):
                total = total + times_row(m, h, sums_of(m, h, range(tiles)))
            return total

        curvature = lax.fori_loop(0, z.no, one_order, curvature)
    curvature = 0.5 * curvature
    adjoint_into(z, func_ref, rows, cols, out_ref)
    out_ref[2 * z.cnt : 2 * z.cnt + 1, :] = jnp.broadcast_to(full_sum(curvature), (1, z.state[1]))
    if not later:
        fetch.wait()


def make_image(z, own, ids, recv, func, state, later):
    vector = jax.ShapeDtypeStruct(z.state, F32)
    table = jax.ShapeDtypeStruct((z.halves, z.table, 128), F32)
    outs = [vector, jax.ShapeDtypeStruct((8, 128), F32)] + ([vector] if later else [table, table])
    outs.append(jax.ShapeDtypeStruct((2, z.halves, z.no, 128), F32))
    if not later:
        outs.append(jax.ShapeDtypeStruct(state[0].shape, F32))
    args = [own, ids, recv, func] + list(state)
    return pl.pallas_call(
        functools.partial(image_kernel, z, later),
        in_specs=[SMEM, SMEM, VMEM, VMEM] + ([VMEM] * len(state) if later else [HBM]),
        out_specs=[VMEM] * len(outs),
        out_shape=outs,
        scratch_shapes=[
            pltpu.VMEM((z.halves, z.pay, 128), F32),
            pltpu.VMEM((z.state[1], 128), F32),
        ]
        + ([] if later else [pltpu.SemaphoreType.DMA((1,))]),
        compiler_params=pltpu.CompilerParams(vmem_limit_bytes=z.limit),
        name="image",
    )(*args)


def last_kernel(z, gathered_ref, energy_ref, res_ref, sol_ref, dir_ref, out_sol, out_res):
    summed, curvature = total_of(z, gathered_ref)
    step_size = energy_ref[0:1, 0:1] / curvature
    sol = sol_ref[...] + step_size * dir_ref[...]
    res = res_ref[...] - step_size * summed
    for slot in range(z.cnt):
        for k in range(2):
            r = k * z.cnt + slot
            out_sol[slot, k : k + 1, :] = sol[r : r + 1, 0 : z.nb]
            out_res[slot, k : k + 1, :] = res[r : r + 1, 0 : z.nb]


def make_last(z, gathered, energy, res, sol, direction):
    out = jax.ShapeDtypeStruct((z.cnt, 2, z.nb), F32)
    return pl.pallas_call(
        functools.partial(last_kernel, z),
        in_specs=[VMEM] * 5,
        out_specs=[VMEM] * 2,
        out_shape=[out, out],
        compiler_params=pltpu.CompilerParams(vmem_limit_bytes=z.limit),
        name="last",
    )(gathered, energy, res, sol, direction)


def body(longitude, cycle_of, obs_count, observed, obs_weight, legendre, precond_inv, order_of_slot):
    z = Sizes(legendre, longitude.shape[1])
    dense = lambda value: pltpu.with_memory_space_constraint(value.reshape(z.rows, 128), pltpu.MemorySpace.HBM)
    held = [dense(value) for value in (longitude, cycle_of, observed, obs_weight)]
    legendre = pltpu.with_memory_space_constraint(legendre, pltpu.MemorySpace.HBM)
    order_of_slot = pltpu.with_memory_space_constraint(order_of_slot, pltpu.MemorySpace.HBM)
    inv = pltpu.with_memory_space_constraint(precond_inv, pltpu.MemorySpace.HBM)
    first = (lax.axis_index("ord") * z.cnt).astype(jnp.int32).reshape(1)
    seeds, *near = make_seeds(z, first, order_of_slot, legendre, held)
    recv = lax.all_to_all(seeds, "ord", 0, 0)
    base = (lax.axis_index("ord") * z.share).astype(jnp.int32).reshape(1)
    sums, ty = make_tables(z, base, obs_count, order_of_slot, *near)
    ids = recv[:, z.id_row, : z.cnt].reshape(z.no).astype(jnp.int32)
    func, part, near_inv = make_functions(z, order_of_slot, recv, ty, inv)
    gathered = lax.all_gather(part, "obs", axis=0)
    values, res, direction = make_step(z, order_of_slot, gathered, near_inv, func, (sums,), False)
    recv = lax.all_to_all(values, "ord", 0, 0)
    part, energy, tc, ts, all_values, near_inv = make_image(z, order_of_slot, ids, recv, func, (inv,), False)
    gathered = lax.all_gather(part, "obs", axis=0)
    values, res, prec, sol = make_step(z, order_of_slot, gathered, near_inv, func, (energy, res, direction), True)
    recv = lax.all_to_all(values, "ord", 0, 0)
    part, energy, direction, all_values = make_image(
        z, order_of_slot, ids, recv, func, (tc, ts, all_values, energy, prec, direction), True
    )
    gathered = lax.all_gather(part, "obs", axis=0)
    return tuple(make_last(z, gathered, energy, res, sol, direction))


def solution(mesh):
    placed = (
        P("obs", None),
        P("obs", None),
        P("obs"),
        P("obs", None),
        P("obs", None),
        P("obs", "ord", None, None),
        P("ord", None, None),
        P("ord"),
    )
    return jax.shard_map(
        body,
        mesh=mesh,
        in_specs=placed,
        out_specs=(P("ord", None, None), P("ord", None, None)),
        check_vma=False,
    )
```

```python
import functools

import jax
import jax.numpy as jnp
from jax import lax
from jax.experimental import pallas as pl
from jax.experimental.pallas import tpu as pltpu
from jax.sharding import PartitionSpec as P

ITERS = 2
SEGMENTS = 2
VMEM_LIMIT = 24 << 20
WINDOW = 32
UNROLL = 8
CHUNK = 1024
F32 = jnp.float32
BF16 = jnp.bfloat16

VMEM = pl.BlockSpec(memory_space=pltpu.VMEM)
SMEM = pl.BlockSpec(memory_space=pltpu.SMEM)
HBM = pl.BlockSpec(memory_space=pltpu.MemorySpace.HBM)


def up(value, unit):
    return -(-value // unit) * unit


def iota(shape, axis):
    return lax.broadcasted_iota(jnp.int32, shape, axis)


class Sizes:
    def __init__(self, legendre, slab):
        self.cnt, self.nb, self.cyc = legendre.shape[1:]
        self.nord = lax.axis_size("ord")
        self.nobs = lax.axis_size("obs")
        self.no = self.cnt * self.nord
        self.slab = slab
        self.rows = slab // 128
        self.halves = self.cyc // 128
        self.steps = self.nb // 8
        self.state = (up(2 * self.cnt + 1, 8), up(self.nb, 128))
        self.seg = SEGMENTS
        self.seg_len = self.nb // SEGMENTS
        self.seed_rows = 2 * self.seg - 1
        self.cos_row = self.cnt * self.seed_rows
        self.id_row = self.cos_row + 1
        self.seeds = up(self.id_row + 1, 8)
        self.pay = up(2 * self.cnt + 1, 8)
        self.off = up(self.no, 8)
        self.share = -(-(2 * self.no - 1) // self.nord)
        self.freq = self.share * self.nord
        self.table = up(self.off + self.freq, 8)
        self.sums = up(2 * (self.share + self.cnt), 16)
        self.spare = self.halves * 2 * self.cnt
        self.sent = up(self.spare + 1, 8)
        self.sent_first = up(self.spare + 1 + self.halves * 2 * self.share, 8)
        self.width = min(CHUNK // 128, self.rows)
        self.chunks = self.rows // self.width
        self.windows = self.cyc // WINDOW
        self.skew = self.rows + 1
        self.seg_skew = self.seg_len + 1
        self.func_rows = up(self.cnt * self.seg * self.seg_skew, 8)
        self.pairs = up(self.chunks + self.windows - 1, UNROLL)
        self.sum_lanes = up(2 * self.sums, 128)
        self.limit = VMEM_LIMIT

    def func_row(self, slot, a):
        segment, at = divmod(8 * a, self.seg_len)
        return (slot * self.seg + segment) * self.seg_skew + at


def send_copies(z, source, out_ref, sems):
    copies = [pltpu.make_async_copy(source, out_ref.at[d], sems.at[d]) for d in range(z.nord)]
    for copy in copies:
        copy.start()
    for copy in copies:
        copy.wait()


def seeds_kernel(z, first_ref, own_ref, leg_ref, *refs):
    held, (out_ref, *near), (stage, keep, sems, out_sems, near_sems) = refs[:4], refs[4:9], refs[9:]
    copies = []

    def fetch(i, at):
        n = len(copies)
        copies.append(pltpu.make_async_copy(leg_ref.at[0, i, pl.ds(at, 8), :], stage.at[n], sems.at[n]))

    for i in range(z.cnt):
        for s in range(1, z.seg):
            fetch(i, s * z.seg_len)
        fetch(i, pl.multiple_of((first_ref[0] + i) // 8 * 8, 8))
    fetch(0, 0)
    for copy in copies:
        copy.start()
    moves = [pltpu.make_async_copy(held[n], near[n], near_sems.at[n]) for n in range(4)]
    for move in moves:
        move.start()
    lane = iota((z.seeds - z.id_row, z.cyc), 1)
    ids = jnp.zeros(lane.shape, F32)
    for slot in range(z.cnt):
        ids = jnp.where(lane == slot, own_ref[slot].astype(F32), ids)
    keep[z.id_row :, :] = ids
    for copy in copies:
        copy.wait()
    for i in range(z.cnt):
        base = i * z.seed_rows
        for s in range(z.seg - 1):
            keep[base + 2 * s : base + 2 * s + 2, :] = stage[i * z.seg + s, 0:2, :]
        order = first_ref[0] + i
        block = stage[i * z.seg + z.seg - 1]
        mine = iota((8, z.cyc), 0) == order - order // 8 * 8
        top = base + z.seed_rows - 1
        keep[top : top + 1, :] = jnp.sum(jnp.where(mine, block, 0.0), axis=0, keepdims=True)
    keep[z.cos_row : z.cos_row + 1, :] = stage[z.cnt * z.seg, 1:2, :]
    send_copies(z, keep, out_ref, out_sems)
    for move in moves:
        move.wait()


def make_seeds(z, first, own, legendre, held):
    slabs = z.cnt * z.seg + 1
    return pl.pallas_call(
        functools.partial(seeds_kernel, z),
        in_specs=[SMEM, SMEM, HBM] + [HBM] * 4,
        out_specs=[HBM] + [VMEM] * 4,
        out_shape=[pltpu.MemorySpace.HBM((z.nord, z.seeds, z.cyc), F32)]
        + [jax.ShapeDtypeStruct(value.shape, value.dtype) for value in held],
        scratch_shapes=[
            pltpu.VMEM((slabs, 8, z.cyc), F32),
            pltpu.VMEM((z.seeds, z.cyc), F32),
            pltpu.SemaphoreType.DMA((slabs,)),
            pltpu.SemaphoreType.DMA((z.nord,)),
            pltpu.SemaphoreType.DMA((4,)),
        ],
        compiler_params=pltpu.CompilerParams(vmem_limit_bytes=z.limit),
        name="seeds",
    )(first, own, legendre, *held)


def sincos(angle):
    turn = jnp.round(angle * 0.6366197723675814)
    rest = angle - turn * 1.5703125
    rest = rest - turn * 4.837512969970703e-4
    rest = rest - turn * 7.549789948768648e-8
    sq = rest * rest
    sine = rest + rest * sq * (-0.16666654611 + sq * (8.3321608736e-3 + sq * -1.9515295891e-4))
    cosine = 1.0 - 0.5 * sq + sq * sq * (4.166664568298827e-2 + sq * (-1.388731625493765e-3 + sq * 2.443315711809948e-5))
    quarter = turn.astype(jnp.int32)
    odd = (quarter & 1) == 1
    c = jnp.where(odd, sine, cosine)
    s = jnp.where(odd, cosine, sine)
    c = jnp.where(((quarter + 1) & 2) == 2, -c, c)
    s = jnp.where((quarter & 2) == 2, -s, s)
    return c, s


def split(value):
    high = value.astype(BF16)
    return high, (value - high.astype(F32)).astype(BF16)


def tables_kernel(z, base_ref, count_ref, own_ref, lon_ref, cyc_ref, data_ref, weight_ref,
                  sum_ref, ty_ref, val, powers, eights, cyc_row, lhs, hot, acc, ids, pair_chunk, pair_window, sems):
    width = z.width
    scalars = [
        pltpu.make_async_copy(cyc_ref.at[pl.ds(c * width, 1), :], ids.at[pl.ds(c, 1), :], sems.at[c])
        for c in range(z.chunks)
    ]
    for copy in scalars:
        copy.start()
    total = z.slab * z.nobs
    size = min(32, z.rows)

    def block(i, carry):
        at = pl.multiple_of(i * size, 8)
        lon = lon_ref[pl.ds(at, size), :]
        place = at * 128 + iota((size, 128), 0) * 128 + iota((size, 128), 1)
        scale = weight_ref[pl.ds(at, size), :] * (place < count_ref[0]).astype(F32) / total
        c1, s1 = sincos(lon)
        c, s = sincos(base_ref[0].astype(F32) * lon)
        c, s = c * scale, s * scale
        for p in range(z.share):
            val[pl.ds(p * z.skew + at, size), :] = c
            val[pl.ds((z.share + p) * z.skew + at, size), :] = s
            c, s = c * c1 - s * s1, s * c1 + c * s1
        scaled = scale * data_ref[pl.ds(at, size), :]
        ones, none = jnp.ones((size, 128), F32), jnp.zeros((size, 128), F32)
        c, s = ones, none
        for p in range(8):
            powers[0, p * size : p * size + size, :] = scaled * c
            powers[1, p * size : p * size + size, :] = scaled * s
            c, s = (c1, s1) if p == 0 else (c * c1 - s * s1, s * c1 + c * s1)
        c8, s8 = c, s
        c, s = ones, none
        for p in range(z.no // 8):
            eights[0, p * size : p * size + size, :] = c
            eights[1, p * size : p * size + size, :] = s
            c, s = (c8, s8) if p == 0 else (c * c8 - s * s8, s * c8 + c * s8)
        for slot in range(z.cnt):
            tens = own_ref[slot] // 8
            small = pl.ds(pl.multiple_of((own_ref[slot] - tens * 8) * size, 8), size)
            large = pl.ds(pl.multiple_of(tens * size, 8), size)
            ca, sa, cb, sb = powers[0, small, :], powers[1, small, :], eights[0, large, :], eights[1, large, :]
            val[pl.ds((2 * z.share + slot) * z.skew + at, size), :] = ca * cb - sa * sb
            val[pl.ds((2 * z.share + z.cnt + slot) * z.skew + at, size), :] = sa * cb + ca * sb
        for row in range(2 * (z.share + z.cnt), z.sums):
            val[pl.ds(row * z.skew + at, size), :] = jnp.zeros((size, 128), F32)
        cyc_row[pl.ds(at, size), :] = cyc_ref[pl.ds(at, size), :].astype(F32)
        return carry

    lax.fori_loop(0, z.rows // size, block, 0)
    acc[...] = jnp.zeros_like(acc)

    def fill(c, carry):
        for k in range(width):
            r = c * width + k
            lanes = slice(k * 128, (k + 1) * 128)
            for pair in range(z.sums // 16):
                first = val[pl.ds(pair * 16 * z.skew + r, 8, stride=z.skew), :]
                second = val[pl.ds((pair * 16 + 8) * z.skew + r, 8, stride=z.skew), :]
                high, low = split(jnp.concatenate([first, second], 0))
                lhs[c, pair * 16 : pair * 16 + 16, lanes] = high
                lhs[c, z.sums + pair * 16 : z.sums + pair * 16 + 16, lanes] = low
        return carry

    lax.fori_loop(0, z.chunks, fill, 0)
    for copy in scalars:
        copy.wait()
    for n in range(z.pairs):
        pair_chunk[n] = 0
        pair_window[n] = z.windows

    def list_chunk(c, count):
        low = ids[c, 0] // WINDOW
        following = ids[jnp.minimum(c + 1, z.chunks - 1), 0] // WINDOW
        high = jnp.where(c + 1 < z.chunks, following, z.windows - 1)

        def add(w, at):
            pair_chunk[at] = c
            pair_window[at] = w
            return at + 1

        return lax.fori_loop(low, high + 1, add, count)

    lax.fori_loop(0, z.chunks, list_chunk, 0)
    cycle_id = iota((WINDOW, 128), 0).astype(F32)

    def some(step, carry):
        for u in range(UNROLL):
            c = pair_chunk[step * UNROLL + u]
            w = pair_window[step * UNROLL + u]
            base = (w * WINDOW).astype(F32)
            for k in range(width):
                here = cyc_row[pl.ds(c * width + k, 1), :] - base
                hot[u, :, k * 128 : (k + 1) * 128] = jnp.where(cycle_id == here, 1.0, 0.0).astype(BF16)
            acc[w] += lax.dot_general(hot[u], lhs[c], (((1,), (1,)), ((), ())), preferred_element_type=F32)
        return carry

    lax.fori_loop(0, z.pairs // UNROLL, some, 0)
    both = 2 * z.share
    per_half = 128 // WINDOW
    for h in range(z.halves):
        flat = jnp.concatenate([acc[h * per_half + w] for w in range(per_half)], 0)
        flat = jnp.concatenate([flat[:, c * 128 : (c + 1) * 128].T for c in range(z.sum_lanes // 128)], 0)
        sum_ref[h, 0:both, :] = flat[0:both] + flat[z.sums : z.sums + both]
        ty_ref[h, 0 : 2 * z.cnt, :] = (
            flat[both : both + 2 * z.cnt] + flat[z.sums + both : z.sums + both + 2 * z.cnt]
        )


def make_tables(z, base, count, own, lon, cyc, data, weight):
    return pl.pallas_call(
        functools.partial(tables_kernel, z),
        in_specs=[SMEM, SMEM, SMEM] + [VMEM] * 4,
        out_specs=[VMEM] * 2,
        out_shape=[
            jax.ShapeDtypeStruct((z.halves, up(2 * z.share, 8), 128), F32),
            jax.ShapeDtypeStruct((z.halves, z.pay, 128), F32),
        ],
        scratch_shapes=[
            pltpu.VMEM((up(z.sums * z.skew, 8), 128), F32),
            pltpu.VMEM((2, 8 * min(32, z.rows), 128), F32),
            pltpu.VMEM((2, z.no // 8 * min(32, z.rows), 128), F32),
            pltpu.VMEM((z.rows, 128), F32),
            pltpu.VMEM((z.chunks, z.sum_lanes, z.width * 128), BF16),
            pltpu.VMEM((UNROLL, WINDOW, z.width * 128), BF16),
            pltpu.VMEM((z.windows + 1, WINDOW, z.sum_lanes), F32),
            pltpu.SMEM((z.chunks, 128), jnp.int32),
            pltpu.SMEM((z.pairs,), jnp.int32),
            pltpu.SMEM((z.pairs,), jnp.int32),
            pltpu.SemaphoreType.DMA((z.chunks,)),
        ],
        compiler_params=pltpu.CompilerParams(vmem_limit_bytes=2 * z.limit),
        name="tables",
    )(base, count, own, lon, cyc, data, weight)


def flip(z, cols_ref, out_ref):
    for c in range(z.state[1] // 128):
        out_ref[:, c * 128 : (c + 1) * 128] = cols_ref[c * 128 : (c + 1) * 128, :].T[0 : z.state[0]]


def adjoint_into(z, func_ref, rows_ref, cols_ref, out_ref):
    cols_ref[...] = jnp.zeros_like(cols_ref)
    for slot in range(z.cnt):
        w = [
            [
                jnp.broadcast_to(rows_ref[h, k * z.cnt + slot : k * z.cnt + slot + 1, :], (8, 128))
                for h in range(z.halves)
            ]
            for k in range(2)
        ]
        for a in range(z.steps):
            f = [func_ref[h, pl.ds(z.func_row(slot, a), 8), :] for h in range(z.halves)]
            for k in range(2):
                prod = f[0] * w[k][0]
                for h in range(1, z.halves):
                    prod = prod + f[h] * w[k][h]
                r = k * z.cnt + slot
                cols_ref[8 * a : 8 * a + 8, r : r + 1] = jnp.sum(prod, axis=1, keepdims=True)
    flip(z, cols_ref, out_ref)


def functions_kernel(z, own_ref, recv_ref, ty_ref, inv_ref, func_ref, out_ref, inv_out, seed0, seed1, first, cols, sem):
    fetch = pltpu.make_async_copy(inv_ref, inv_out, sem.at[0])
    fetch.start()
    total = z.seg * z.cnt
    padded = up(total, 8)
    for slot in range(z.cnt):
        order = own_ref[slot]
        block = order // z.cnt
        base = (order - block * z.cnt) * z.seed_rows
        for s in range(z.seg):
            r = slot * z.seg + s
            if s > 0:
                seed0[r : r + 1, :] = recv_ref[block, pl.ds(base + 2 * s - 2, 1), :]
                seed1[r : r + 1, :] = recv_ref[block, pl.ds(base + 2 * s - 1, 1), :]
            else:
                seed0[r : r + 1, :] = jnp.zeros((1, z.cyc), F32)
                seed1[r : r + 1, :] = jnp.zeros((1, z.cyc), F32)
            first[r : r + 1, :] = recv_ref[block, pl.ds(base + z.seed_rows - 1, 1), :]
    ground = recv_ref[0, z.seed_rows - 1 : z.seed_rows, :]
    cosine = recv_ref[0, z.cos_row : z.cos_row + 1, :] / (ground * 1.7320508075688772)
    lanes_len = up(z.seg_len, 128)
    row = iota((padded, lanes_len), 0)
    order_of = jnp.zeros(row.shape, F32)
    start_of = jnp.zeros(row.shape, F32)
    for slot in range(z.cnt):
        for s in range(z.seg):
            hit = row == slot * z.seg + s
            order_of = jnp.where(hit, own_ref[slot].astype(F32), order_of)
            start_of = jnp.where(hit, float(s * z.seg_len), start_of)
    degree = start_of + iota(row.shape, 1).astype(F32)
    minus = jnp.maximum(degree - order_of, 1.0)
    plus = jnp.maximum(degree + order_of, 1.0)
    rise = jnp.sqrt(jnp.maximum((2.0 * degree - 1.0) * (2.0 * degree + 1.0), 0.0) / (minus * plus))
    rise = jnp.where(degree > order_of, rise, 0.0)
    top = jnp.maximum((2.0 * degree + 1.0) * (degree + order_of - 1.0) * (degree - order_of - 1.0), 0.0)
    fall = jnp.sqrt(top / (minus * plus * jnp.maximum(2.0 * degree - 3.0, 1.0)))
    fall = jnp.where(degree > order_of + 1.0, fall, 0.0)
    for tile in range(padded // 8):
        rows = slice(tile * 8, tile * 8 + 8)
        left = min(8, total - tile * 8)
        entry = order_of[rows, 0:128] - start_of[rows, 0:128]
        lowest = start_of[rows, 0:128] == 0.0
        now, prev, before = [None] * z.halves, [None] * z.halves, [None] * z.halves
        for t in range(z.seg_len):
            if t > 0:
                up_by = jnp.broadcast_to(rise[rows, t : t + 1], (8, 128))
                down_by = jnp.broadcast_to(fall[rows, t : t + 1], (8, 128))
            here = entry == float(t)
            for h in range(z.halves):
                lanes = slice(h * 128, (h + 1) * 128)
                x = jnp.broadcast_to(cosine[:, lanes], (8, 128))
                if t == 0:
                    value = seed0[rows, lanes]
                elif t == 1:
                    value = jnp.where(lowest, (up_by * x) * prev[h], seed1[rows, lanes])
                else:
                    value = (up_by * x) * prev[h] - down_by * before[h]
                now[h] = jnp.where(here, first[rows, lanes], value)
                func_ref[h, pl.ds(tile * 8 * z.seg_skew + t, left, stride=z.seg_skew), :] = now[h][:left]
            before, prev, now = prev, now, [None] * z.halves
    adjoint_into(z, func_ref, ty_ref, cols, out_ref)
    fetch.wait()


def make_functions(z, own, recv, ty, inv):
    padded = up(z.seg * z.cnt, 8)
    return pl.pallas_call(
        functools.partial(functions_kernel, z),
        in_specs=[SMEM, VMEM, VMEM, HBM],
        out_specs=[VMEM] * 3,
        out_shape=[
            jax.ShapeDtypeStruct((z.halves, z.func_rows, 128), F32),
            jax.ShapeDtypeStruct(z.state, F32),
            jax.ShapeDtypeStruct(inv.shape, F32),
        ],
        scratch_shapes=[pltpu.VMEM((padded, z.cyc), F32)] * 3
        + [pltpu.VMEM((z.state[1], 128), F32), pltpu.SemaphoreType.DMA((1,))],
        compiler_params=pltpu.CompilerParams(vmem_limit_bytes=z.limit),
        name="functions",
    )(own, recv, ty, inv)


def total_of(z, gathered_ref):
    summed = gathered_ref[0]
    for b in range(1, gathered_ref.shape[0]):
        summed = summed + gathered_ref[b]
    return summed, summed[2 * z.cnt : 2 * z.cnt + 1, 0:1]


def full_sum(value):
    return jnp.sum(jnp.sum(value, axis=1, keepdims=True), axis=0, keepdims=True)


def step_kernel(z, later, own_ref, *refs):
    if later:
        gathered_ref, inv_ref, func_ref, energy_ref, res_ref, dir_ref = refs[:6]
        out_ref, newres_ref, prec_ref, sol_ref, cols, pay, sems = refs[6:]
    else:
        gathered_ref, inv_ref, func_ref, sum_ref = refs[:4]
        out_ref, newres_ref, prec_ref, cols, pay, sems = refs[4:]
    summed, curvature = total_of(z, gathered_ref)
    if later:
        step_size = energy_ref[0:1, 0:1] / curvature
        sol_ref[...] = step_size * dir_ref[...]
        newres_ref[...] = res_ref[...] - step_size * summed
    else:
        newres_ref[...] = summed
    cols[...] = jnp.zeros_like(cols)
    height = iota((8, 128), 0)
    for slot in range(z.cnt):
        vec = [
            jnp.broadcast_to(newres_ref[k * z.cnt + slot : k * z.cnt + slot + 1, 0 : z.nb], (8, z.nb)) for k in range(2)
        ]
        acc = [[jnp.zeros((8, 128), F32)] * z.halves for k in range(2)]
        for a in range(z.steps):
            block = inv_ref[slot, 8 * a : 8 * a + 8, :]
            live = height >= own_ref[slot] - 8 * a
            f = [func_ref[h, pl.ds(z.func_row(slot, a), 8), :] for h in range(z.halves)]
            for k in range(2):
                r = k * z.cnt + slot
                col = jnp.broadcast_to(jnp.sum(block * vec[k], axis=1, keepdims=True), (8, 128))
                col = jnp.where(live, col, 0.0)
                cols[8 * a : 8 * a + 8, r : r + 1] = col[:, r : r + 1]
                for h in range(z.halves):
                    acc[k][h] = acc[k][h] + f[h] * col
        for k in range(2):
            r = k * z.cnt + slot
            for h in range(z.halves):
                pay[h * 2 * z.cnt + r : h * 2 * z.cnt + r + 1, :] = jnp.sum(acc[k][h], axis=0, keepdims=True)
    flip(z, cols, prec_ref)
    top = z.spare + 1
    pay[z.spare : top, :] = jnp.broadcast_to(full_sum(newres_ref[...] * prec_ref[...]), (1, 128))
    if not later:
        for h in range(z.halves):
            at = top + h * 2 * z.share
            pay[at : at + 2 * z.share, :] = sum_ref[h, 0 : 2 * z.share, :]
    send_copies(z, pay, out_ref, sems)


def make_step(z, own, gathered, inv, func, state, later):
    vector = jax.ShapeDtypeStruct(z.state, F32)
    outs = [pltpu.MemorySpace.HBM((z.nord, z.sent if later else z.sent_first, 128), F32)] + [vector] * (2 + later)
    args = [own, gathered, inv, func] + list(state)
    return pl.pallas_call(
        functools.partial(step_kernel, z, later),
        in_specs=[SMEM] + [VMEM] * (len(args) - 1),
        out_specs=[HBM] + [VMEM] * (len(outs) - 1),
        out_shape=outs,
        scratch_shapes=[
            pltpu.VMEM((z.state[1], 128), F32),
            pltpu.VMEM(outs[0].shape[1:], F32),
            pltpu.SemaphoreType.DMA((z.nord,)),
        ],
        compiler_params=pltpu.CompilerParams(vmem_limit_bytes=z.limit),
        name="step",
    )(*args)


def image_kernel(z, later, own_ref, ids_ref, recv_ref, func_ref, *refs):
    if later:
        tc_ref, ts_ref, old_ref, old_energy_ref, prec_ref, old_dir_ref = refs[:6]
        out_ref, energy_ref, dir_ref, val_ref, rows, cols = refs[6:]
    else:
        inv_ref, out_ref, energy_ref, tc_ref, ts_ref, val_ref, inv_out, rows, cols, sem = refs
        fetch = pltpu.make_async_copy(inv_ref, inv_out, sem.at[0])
        fetch.start()
        for o in range(z.nord):
            at = z.off + o * z.share
            for h in range(z.halves):
                top = z.spare + 1 + h * 2 * z.share
                tc_ref[h, at : at + z.share, :] = recv_ref[o, top : top + z.share, :]
                ts_ref[h, at : at + z.share, :] = recv_ref[o, top + z.share : top + 2 * z.share, :]

        def mirror(q, carry):
            for h in range(z.halves):
                tc_ref[h, pl.ds(z.off - q, 1), :] = tc_ref[h, pl.ds(z.off + q, 1), :]
                ts_ref[h, pl.ds(z.off - q, 1), :] = -ts_ref[h, pl.ds(z.off + q, 1), :]
            return carry

        lax.fori_loop(1, z.no, mirror, 0)
    energy = recv_ref[0, z.spare : z.spare + 1, :]
    for o in range(1, z.nord):
        energy = energy + recv_ref[o, z.spare : z.spare + 1, :]
    energy_ref[...] = jnp.broadcast_to(energy, (8, 128))

    def place(o, carry):
        for i in range(z.cnt):
            order = ids_ref[o * z.cnt + i]
            for k in range(2):
                for h in range(z.halves):
                    r = (h * 2 + k) * z.cnt + i
                    val_ref[k, h, pl.ds(order, 1), :] = recv_ref[o, r : r + 1, :]
        return carry

    lax.fori_loop(0, z.nord, place, 0)
    if later:
        ratio = energy / old_energy_ref[0:1, :]
        for k in range(2):
            for h in range(z.halves):
                val_ref[k, h] = val_ref[k, h] + ratio * old_ref[k, h]
        dir_ref[...] = prec_ref[...] + ratio[:, 0:1] * old_dir_ref[...]

    tiles = z.no // 8

    def sums_of(m, h, chosen):
        both = None
        for tile in chosen:
            vc, vs = val_ref[0, h, tile * 8 : tile * 8 + 8, :], val_ref[1, h, tile * 8 : tile * 8 + 8, :]
            low, high = pl.ds(z.off + tile * 8 - m, 8), pl.ds(z.off + tile * 8 + m, 8)
            near, far = tc_ref[h, low, :], tc_ref[h, high, :]
            snear, sfar = ts_ref[h, low, :], ts_ref[h, high, :]
            wc = (near + far) * vc + (sfar + snear) * vs
            ws = (sfar - snear) * vc + (near - far) * vs
            both = (wc, ws) if both is None else (both[0] + wc, both[1] + ws)
        return both

    for i in range(z.cnt):
        for h in range(z.halves):
            for k, value in enumerate(sums_of(own_ref[i], h, range(tiles))):
                r = k * z.cnt + i
                rows[h, r : r + 1, :] = 0.5 * jnp.sum(value, axis=0, keepdims=True)

    def times_row(m, h, value):
        at = pl.ds(m, 1)
        return val_ref[0, h, at, :] * value[0] + val_ref[1, h, at, :] * value[1]

    curvature = jnp.zeros((8, 128), F32)
    if z.no <= 128:
        for m in range(z.no):
            for h in range(z.halves):
                value = sums_of(m, h, [m // 8])
                if m // 8 + 1 < tiles:
                    above = sums_of(m, h, range(m // 8 + 1, tiles))
                    value = [v + 2.0 * w for v, w in zip(value, above)]
                curvature = curvature + times_row(m, h, value)
    else:

        def one_order(m, total):
            for h in range(z.halves):
                total = total + times_row(m, h, sums_of(m, h, range(tiles)))
            return total

        curvature = lax.fori_loop(0, z.no, one_order, curvature)
    curvature = 0.5 * curvature
    adjoint_into(z, func_ref, rows, cols, out_ref)
    out_ref[2 * z.cnt : 2 * z.cnt + 1, :] = jnp.broadcast_to(full_sum(curvature), (1, z.state[1]))
    if not later:
        fetch.wait()


def make_image(z, own, ids, recv, func, state, later):
    vector = jax.ShapeDtypeStruct(z.state, F32)
    table = jax.ShapeDtypeStruct((z.halves, z.table, 128), F32)
    outs = [vector, jax.ShapeDtypeStruct((8, 128), F32)] + ([vector] if later else [table, table])
    outs.append(jax.ShapeDtypeStruct((2, z.halves, z.no, 128), F32))
    if not later:
        outs.append(jax.ShapeDtypeStruct(state[0].shape, F32))
    args = [own, ids, recv, func] + list(state)
    return pl.pallas_call(
        functools.partial(image_kernel, z, later),
        in_specs=[SMEM, SMEM, VMEM, VMEM] + ([VMEM] * len(state) if later else [HBM]),
        out_specs=[VMEM] * len(outs),
        out_shape=outs,
        scratch_shapes=[
            pltpu.VMEM((z.halves, z.pay, 128), F32),
            pltpu.VMEM((z.state[1], 128), F32),
        ]
        + ([] if later else [pltpu.SemaphoreType.DMA((1,))]),
        compiler_params=pltpu.CompilerParams(vmem_limit_bytes=z.limit),
        name="image",
    )(*args)


def last_kernel(z, gathered_ref, energy_ref, res_ref, sol_ref, dir_ref, out_sol, out_res):
    summed, curvature = total_of(z, gathered_ref)
    step_size = energy_ref[0:1, 0:1] / curvature
    sol = sol_ref[...] + step_size * dir_ref[...]
    res = res_ref[...] - step_size * summed
    for slot in range(z.cnt):
        for k in range(2):
            r = k * z.cnt + slot
            out_sol[slot, k : k + 1, :] = sol[r : r + 1, 0 : z.nb]
            out_res[slot, k : k + 1, :] = res[r : r + 1, 0 : z.nb]


def make_last(z, gathered, energy, res, sol, direction):
    out = jax.ShapeDtypeStruct((z.cnt, 2, z.nb), F32)
    return pl.pallas_call(
        functools.partial(last_kernel, z),
        in_specs=[VMEM] * 5,
        out_specs=[VMEM] * 2,
        out_shape=[out, out],
        compiler_params=pltpu.CompilerParams(vmem_limit_bytes=z.limit),
        name="last",
    )(gathered, energy, res, sol, direction)


def over_obs(z, part):
    if z.nobs & (z.nobs - 1):
        return lax.all_gather(part, "obs", axis=0)
    bit = 1
    while bit < z.nobs // 2:
        part = part + lax.ppermute(part, "obs", [(i, i ^ bit) for i in range(z.nobs)])
        bit *= 2
    return (part + lax.ppermute(part, "obs", [(i, i ^ bit) for i in range(z.nobs)]))[None]


def body(longitude, cycle_of, obs_count, observed, obs_weight, legendre, precond_inv, order_of_slot):
    z = Sizes(legendre, longitude.shape[1])
    dense = lambda value: pltpu.with_memory_space_constraint(value.reshape(z.rows, 128), pltpu.MemorySpace.HBM)
    held = [dense(value) for value in (longitude, cycle_of, observed, obs_weight)]
    legendre = pltpu.with_memory_space_constraint(legendre, pltpu.MemorySpace.HBM)
    order_of_slot = pltpu.with_memory_space_constraint(order_of_slot, pltpu.MemorySpace.HBM)
    inv = pltpu.with_memory_space_constraint(precond_inv, pltpu.MemorySpace.HBM)
    first = (lax.axis_index("ord") * z.cnt).astype(jnp.int32).reshape(1)
    seeds, *near = make_seeds(z, first, order_of_slot, legendre, held)
    recv = lax.all_to_all(seeds, "ord", 0, 0)
    base = (lax.axis_index("ord") * z.share).astype(jnp.int32).reshape(1)
    sums, ty = make_tables(z, base, obs_count, order_of_slot, *near)
    ids = recv[:, z.id_row, : z.cnt].reshape(z.no).astype(jnp.int32)
    func, part, near_inv = make_functions(z, order_of_slot, recv, ty, inv)
    gathered = over_obs(z, part)
    values, res, direction = make_step(z, order_of_slot, gathered, near_inv, func, (sums,), False)
    recv = lax.all_to_all(values, "ord", 0, 0)
    part, energy, tc, ts, all_values, near_inv = make_image(z, order_of_slot, ids, recv, func, (inv,), False)
    gathered = over_obs(z, part)
    values, res, prec, sol = make_step(z, order_of_slot, gathered, near_inv, func, (energy, res, direction), True)
    recv = lax.all_to_all(values, "ord", 0, 0)
    part, energy, direction, all_values = make_image(
        z, order_of_slot, ids, recv, func, (tc, ts, all_values, energy, prec, direction), True
    )
    gathered = over_obs(z, part)
    return tuple(make_last(z, gathered, energy, res, sol, direction))


def solution(mesh):
    placed = (
        P("obs", None),
        P("obs", None),
        P("obs"),
        P("obs", None),
        P("obs", None),
        P("obs", "ord", None, None),
        P("ord", None, None),
        P("ord"),
    )
    return jax.shard_map(
        body,
        mesh=mesh,
        in_specs=placed,
        out_specs=(P("ord", None, None), P("ord", None, None)),
        check_vma=False,
    )
```
